512 devices in a mesh: pipe: 16 (over z, core), expert: 8 (over y), dp: 4 (over x).
Axes of the slice: x: 4, y: 8, z: 8, core: 2. Of those that a mesh axis runs over, the one named last changes fastest.
Arguments:
- tokens: bfloat16 [8, 8, 16, 6144], P(None, 'expert', None, 'dp'), may hold values from -8 to 8
- norm_gain: float32 [6144], P('dp'), may hold values from 0.5 to 1.5
- up_w: bfloat16 [8, 6144, 8192], P('expert', 'dp', 'pipe'), may hold values from -0.078125 to 0.078125
- down_w: bfloat16 [8, 8192, 6144], P('expert', 'pipe', 'dp'), may hold values from -0.0625 to 0.0625
- expert_ids: int32 [8, 8, 16, 2], P(None, 'expert'), may hold values from 0 to 7, all different within a row; in each aligned block of 16 rows (0 to 15, 16 to 31, ..., all dimensions but the last counted through in order) at most 6 rows name the same one
- gate_gap: float32 [8, 8, 16], P(None, 'expert'), may hold values from 0 to 2.5
Outputs:
- result: bfloat16 [8, 8, 16, 6144], P(None, 'expert', None, ('dp', 'pipe'))
The draws below stay inside these ranges and needn't reach their ends.
Inputs may be any that keep to these rules, and one draw needn't show every extreme that they name: `expert_ids`: each token names 2 different experts. Of the 16 tokens of one micro-batch and one index along the second dimension (an aligned block of 16 rows), at most 6 name any one expert.
All inputs are finite; a program needn't handle non-finite values.
Results may differ from the reference program's by a relative error of at most 0.0095.
Values may be sent and summed in bfloat16 or wider, within the bound.
A program may use at most 64 MiB of HBM per device.

```python
import math
import jax
import jax.numpy as jnp
import numpy as np
from jax import lax

D = 6144
EXPERTS = 8
TOPK = 2
UNITS = 8192
SECTION = 512
ROWS = 16
MICRO = 8
CAP = 6


def draw_tokens(key, part):
    key_base = jax.random.fold_in(jax.random.fold_in(key, 11), 0)
    shape = (MICRO, EXPERTS, ROWS, D)
    feature = jnp.arange(D, dtype=jnp.float32) / jnp.float32(max(D - 1, 1))
    base = jax.random.normal(key_base, shape, jnp.float32)
    column = jnp.exp(jnp.log(3.0) * (feature - 0.5))
    values = base * column
    return jnp.clip(values, -8.0, 8.0).astype(jnp.bfloat16)


def block_scale(rng, dims, cuts, least, top_value):
    level, own = 1.0, jax.random.fold_in(rng, 6)
    for axis_at, shards_of in cuts:
        heights = jnp.exp(jax.random.uniform(jax.random.fold_in(own, axis_at), (shards_of,), jnp.float32, least / len(cuts), top_value / len(cuts)))
        level = level * jnp.repeat(heights, dims[axis_at] // shards_of).reshape([-1 if axis == axis_at else 1 for axis in range(len(dims))])
    return level


def shared_out(stream_key, own, number, rows, count, top, bound, lean):
    sequence = jax.random.permutation(stream_key, count)
    crowded, common = shares(count, rows * top, bound, lean, True), shares(count, rows * top, bound, lean, False)
    places = jnp.arange(count)

    def named(lengths, turn):
        used = int((lengths > 0).sum())
        fixed = max(1, used // 4)
        moved = fixed + (places - fixed + turn * (used - fixed)) % max(1, count - fixed)
        return jnp.zeros((count,), jnp.int32).at[sequence[jnp.where(places < fixed, places, moved)]].set(jnp.asarray(lengths, jnp.int32))

    lengths = jnp.where(number % 4 == 0, named(crowded, number // 4), named(common, number - number // 4 - 1))
    mixed = jax.random.permutation(jax.random.fold_in(own, 3), count)
    source_of, taker = mixed[0:count // 2 * 2:2], mixed[1:count // 2 * 2:2]
    margin = jnp.minimum(lengths[source_of] - 1, bound - lengths[taker]) // 2
    margin = jnp.where((source_of == sequence[0]) | (taker == sequence[0]) | (lengths[taker] == 0), 0, jnp.maximum(margin, 0))
    moved = jax.random.randint(jax.random.fold_in(own, 4), (count // 2,), 0, 1 << 20) % (margin + 1)
    lengths = lengths.at[source_of].add(-moved).at[taker].add(moved)
    labels = jnp.searchsorted(jnp.cumsum(lengths), jnp.arange(rows * top), side="right").astype(jnp.int32)
    table = labels.reshape(top, rows).T
    table = table[jax.random.permutation(jax.random.fold_in(own, 1), rows)]
    turn = jax.random.randint(jax.random.fold_in(own, 2), (rows, 1), 0, top)
    return jnp.take_along_axis(table, (jnp.arange(top)[None, :] + turn) % top, axis=1)


def shares(number_of, total, most, skew, full):
    loads = [(1 << 20) // math.isqrt(standing ** skew) + 1 for standing in range(1, number_of + 1)]
    largest = most if full else min(most, max(-(-total // number_of), total * loads[0] // sum(loads)))
    least = 1 if total - largest >= number_of - 1 else 0
    given, spare = [largest] + [least] * (number_of - 1), total - largest - least * (number_of - 1)
    while spare > 0:
        candidates = [i for i in range(1, number_of) if given[i] < largest] or [i for i in range(1, number_of) if given[i] < most]
        mass, remaining = sum([loads[i] for i in candidates]), spare
        for i in candidates:
            addition = min(most - given[i], max(1, remaining * loads[i] // mass), spare)
            given[i] = given[i] + addition
            spare = spare - addition
    return np.array(given)


def centred(own_key, dims, deviation, most, pieces=(), kind=jnp.bfloat16):
    values = jax.random.normal(own_key, dims, jnp.float32) * deviation
    if len(pieces) > 0:
        values = block_scale(own_key, dims, pieces, -0.22, 0.18) * values
    return jnp.clip(values, min=-most, max=most).astype(kind)


def setup_inputs(seed: int = 0) -> dict:
    seeds = jax.random.split(jax.random.key(seed), 7)
    tokens = draw_tokens(jax.random.fold_in(seeds[6], 71), 0)
    norm_gain = jnp.clip(0.5 + 1.0 * jax.random.uniform(seeds[1], (D,), jnp.float32) ** block_scale(seeds[1], (D,), ((0, 4),), -0.2, 0.2), 0.5, 1.5)
    up_w = centred(seeds[2], (EXPERTS, D, UNITS), D ** -0.5, 0.078125, ((0, 8), (1, 4), (2, 16)))
    down_w = centred(seeds[3], (EXPERTS, UNITS, D), UNITS ** -0.5, 0.0625, ((0, 8), (1, 16), (2, 4)))
    expert_ids_keys = jax.random.split(jax.random.fold_in(seeds[4], 1), MICRO * EXPERTS * ROWS // ROWS)
    expert_ids_turns = jax.random.permutation(jax.random.fold_in(seeds[4], 3), MICRO * EXPERTS * ROWS // ROWS)
    expert_ids = jax.vmap(lambda own, number: shared_out(jax.random.fold_in(seeds[4], 2), own, number, ROWS, EXPERTS, TOPK, CAP, 2))(expert_ids_keys, expert_ids_turns).reshape((MICRO, EXPERTS, ROWS, TOPK))
    gate_gap = jnp.clip(2.5 * jax.random.uniform(seeds[5], (MICRO, EXPERTS, ROWS), jnp.float32) ** block_scale(seeds[5], (MICRO, EXPERTS, ROWS), ((1, 8),), -0.2, 0.2), 0.0, 2.5)
    return dict(tokens=tokens, norm_gain=norm_gain, up_w=up_w, down_w=down_w, expert_ids=expert_ids, gate_gap=gate_gap)


def reference(tokens, norm_gain, up_w, down_w, expert_ids, gate_gap):
    all_rows = MICRO * EXPERTS * ROWS
    state = tokens.reshape(all_rows, D).astype(jnp.float32)
    scale_rows = lax.rsqrt(lax.optimization_barrier(jnp.mean(state * state, axis=-1, keepdims=True)) + 1e-05)
    normed = (state * scale_rows * norm_gain).astype(jnp.bfloat16)
    route_ids = expert_ids.reshape(all_rows, TOPK)
    first_share = jax.nn.sigmoid(gate_gap.reshape(all_rows).astype(jnp.float32))
    limit = MICRO * EXPERTS * CAP
    sections = UNITS // SECTION

    def per_expert(expert, total):
        member = (route_ids[:, 0] == expert) | (route_ids[:, 1] == expert)
        picked = jnp.nonzero(member, size=limit, fill_value=0)[0]
        valid = jnp.arange(limit) < jnp.sum(member.astype(jnp.int32))
        weight = jnp.where(route_ids[:, 0] == expert, first_share, jnp.float32(0.0))
        weight = weight + jnp.where(route_ids[:, 1] == expert, jnp.float32(1.0) - first_share, jnp.float32(0.0))
        weight_sel = jnp.where(valid, weight[picked], jnp.float32(0.0))
        rows_in = normed[picked]
        w_up = lax.dynamic_index_in_dim(up_w, expert, 0, keepdims=False)
        hidden = jax.nn.silu(jnp.dot(rows_in, w_up, preferred_element_type=jnp.float32)).astype(jnp.bfloat16)
        w_down = lax.dynamic_index_in_dim(down_w, expert, 0, keepdims=False).astype(jnp.float32).reshape(sections, SECTION, D)
        parts = jnp.einsum('nsu,sud->nsd', hidden.astype(jnp.float32).reshape(limit, sections, SECTION), w_down)
        parts = lax.optimization_barrier(parts.astype(jnp.bfloat16)).astype(jnp.float32)
        expert_out = lax.optimization_barrier(jnp.sum(parts, axis=1))
        return total.at[picked].add(weight_sel[:, None] * expert_out)
    summed = lax.fori_loop(0, EXPERTS, per_expert, jnp.zeros((all_rows, D), jnp.float32))
    return (state + summed).astype(jnp.bfloat16).reshape(MICRO, EXPERTS, ROWS, D)
```

```python
import jax
import jax.numpy as jnp
from jax import lax
from jax.experimental import pallas as pl
from jax.experimental.pallas import tpu as pltpu
from jax.sharding import PartitionSpec as P

MESH = pl.DeviceIdType.MESH
OFFSETS = (0, 1, -1, 2, -2, 3, -3, 4)
GROUPS = 2
SLOTS = 8
PER = 4
CAP = 6
F32 = jnp.float32
BF16 = jnp.bfloat16


def layer_kernel(
    tok_ref, gain_ref, meta_ref, up_hbm, down_hbm, out_ref,
    wu, wd, pk, xg, xn, rs, rr, hb, cs, cr, zs, zr, ys, ret, pwh, pwl,
    w_sem, a_s, a_r, b_s, b_r, c_s, c_r, d_s, d_r, e_s, e_r, f_s, f_r, g_s, g_r,
):
    p = lax.axis_index("pipe")
    y = lax.axis_index("expert")
    x = lax.axis_index("dp")
    n_y = lax.axis_size("expert")
    n_x = lax.axis_size("dp")
    n_z = lax.axis_size("pipe") // 2
    z = p // 2
    c = p % 2
    partner = 2 * z + 1 - c
    n_tok, width = tok_ref.shape
    half = width // 2
    rows = pk.shape[1]
    units = wu.shape[1]
    feats = width // (2 * n_z)
    lane_group = PER * feats

    def dev_y(offset):
        return (p, lax.rem(y + offset + n_y, n_y), x)

    def dev_x(j):
        return (p, y, lax.rem(x + j, n_x))

    def dev_z(j):
        return (2 * lax.rem(z + j, n_z) + c, y, x)

    def remote(src, dst, s, r, dev):
        return pltpu.make_async_remote_copy(
            src_ref=src, dst_ref=dst, send_sem=s, recv_sem=r, device_id=dev, device_id_type=MESH
        )

    weight_copies = [pltpu.make_async_copy(up_hbm, wu, w_sem.at[0])]
    for part in range(wd.shape[0]):
        weight_copies.append(
            pltpu.make_async_copy(
                down_hbm.at[:, pl.ds(part * lane_group, lane_group)], wd.at[part], w_sem.at[1 + part]
            )
        )
    for copy in weight_copies:
        copy.start()

    barrier = pltpu.get_barrier_semaphore()
    peers = [dev_y(o) for o in OFFSETS[1:]] + [dev_x(j) for j in range(1, 4)]
    peers += [dev_z(j) for j in range(1, 8)] + [(partner, y, x)]
    for dev in peers:
        pl.semaphore_signal(barrier, inc=1, device_id=dev, device_id_type=MESH)

    sub = lax.broadcasted_iota(jnp.int32, (SLOTS, n_tok), 0)
    lane = lax.broadcasted_iota(jnp.int32, (SLOTS, n_tok), 1)
    offset = jnp.zeros_like(sub)
    for k in range(SLOTS):
        offset = jnp.where(sub == k, OFFSETS[k], offset)
    expert_of = y - offset
    expert_of = jnp.where(expert_of < 0, expert_of + n_y, expert_of)
    expert_of = jnp.where(expert_of >= n_y, expert_of - n_y, expert_of).astype(F32)
    first = meta_ref[0:1, :] == expert_of
    second = meta_ref[1:2, :] == expert_of
    share = 1.0 / (1.0 + jnp.exp(-meta_ref[2:3, :]))
    weight = jnp.where(first, share, 0.0) + jnp.where(second, 1.0 - share, 0.0)
    member = first | second
    before = lax.broadcasted_iota(jnp.int32, (n_tok, n_tok), 0)
    token = lax.broadcasted_iota(jnp.int32, (n_tok, n_tok), 1)
    block_of = (token // 16) == (before // 16)
    earlier = jnp.where(block_of & (before < token), 1.0, 0.0).astype(BF16)
    rank = jnp.dot(jnp.where(member, 1.0, 0.0).astype(BF16), earlier, preferred_element_type=F32)
    code = jnp.where(member, rank + ((lane // 16) * CAP).astype(F32), -1.0)
    row_id = lax.broadcasted_iota(jnp.int32, (rows, n_tok), 0).astype(F32)
    lo_half = pl.multiple_of(c * half, 128)
    own_half = tok_ref[:, pl.ds(lo_half, half)]
    for k in range(SLOTS):
        hit = code[k : k + 1, :] == row_id
        pick = jnp.where(hit, 1.0, 0.0).astype(BF16)
        if k == 0:
            both = jnp.dot(pick, tok_ref[...], preferred_element_type=F32).astype(BF16)
            xg[0, 0] = both[:, :half]
            xg[1, 0] = both[:, half:]
        else:
            pk[k] = jnp.dot(pick, own_half, preferred_element_type=F32).astype(BF16)

    pl.semaphore_wait(barrier, len(peers))

    a_copies = [None]
    for k in range(1, SLOTS):
        copy = remote(pk.at[k], xg.at[c, k], a_s.at[k], a_r.at[k], dev_y(-OFFSETS[k]))
        copy.start()
        a_copies.append(copy)

    for k in range(SLOTS):
        hit = code[k : k + 1, :] == row_id
        placed = jnp.where(hit, weight[k : k + 1, :], 0.0)
        high = placed.astype(BF16)
        pwh[pl.ds(k * rows, rows), :] = high
        pwl[pl.ds(k * rows, rows), :] = (placed - high.astype(F32)).astype(BF16)

    b_copies = {}
    c_copies, d_copies, e_copies, f_copies, g_copies = {}, {}, {}, {}, {}

    def prepare(g, q, k, h, total):
        lo = pl.multiple_of(h * half, 128) if not isinstance(h, int) else h * half
        block = xg[h, k].astype(F32)
        total = total + jnp.sum(block * block, axis=-1, keepdims=True)
        xn[g, pl.ds(q * rows, rows), pl.ds(lo, half)] = (block * gain_ref[:, pl.ds(lo, half)]).astype(BF16)
        return total

    def stage_a(g):
        totals = []
        for q in range(PER):
            k = g * PER + q
            total = jnp.zeros((rows, 1), F32)
            if k > 0:
                a_copies[k].wait_recv()
                b_copies[k] = remote(xg.at[c, k], xg.at[c, k], b_s.at[k], b_r.at[k], (partner, y, x))
                b_copies[k].start()
                total = prepare(g, q, k, c, total)
            else:
                total = prepare(g, q, k, 0, total)
                total = prepare(g, q, k, 1, total)
            totals.append(total)
        for q in range(PER):
            k = g * PER + q
            if k > 0:
                b_copies[k].wait_recv()
                totals[q] = prepare(g, q, k, 1 - c, totals[q])
        if g == 0:
            weight_copies[0].wait()
        gate = jnp.dot(xn[g], wu[...], preferred_element_type=F32)
        lanes = lax.broadcasted_iota(jnp.int32, (rows, 128), 1)
        for q in range(PER):
            rs[g, q, :, pl.ds(0, units)] = gate[q * rows : (q + 1) * rows].astype(BF16)
            square = jnp.broadcast_to(totals[q], (rows, 128))
            high = square.astype(BF16).astype(F32)
            rs[g, q, :, pl.ds(units, 128)] = jnp.where(lanes < 64, high, square - high).astype(BF16)
        for j in range(1, 4):
            copy = remote(rs.at[g, lax.rem(x + j, n_x)], rr.at[g, j], c_s.at[g, j], c_r.at[g, j], dev_x(j))
            copy.start()
            c_copies[g, j] = copy

    def stage_b(g):
        total = rs[g, x].astype(F32)
        for j in range(1, 4):
            c_copies[g, j].wait_recv()
            total = total + rr[g, j].astype(F32)
        square = total[:, units : units + 1] + total[:, units + 64 : units + 65]
        scale = lax.rsqrt(square / (width * n_x) + 1e-05)
        gate = total[:, :units] * scale
        hb[g, x] = (gate / (1.0 + jnp.exp(-gate))).astype(BF16)
        for j in range(1, 4):
            copy = remote(hb.at[g, x], hb.at[g, x], d_s.at[g, j], d_r.at[g, j], dev_x(j))
            copy.start()
            d_copies[g, j] = copy

    def stage_c(g):
        for j in range(1, 4):
            d_copies[g, j].wait_recv()
        hidden = hb[g].reshape(PER * rows, units)
        if g == 0:
            for copy in weight_copies[1:]:
                copy.wait()
        lanes = lax.broadcasted_iota(jnp.int32, (rows, lane_group), 1)
        for part in range(wd.shape[0]):
            outs = jnp.dot(hidden, wd[part], preferred_element_type=F32)
            for r in range(PER):
                packed = None
                for q in range(PER):
                    piece = outs[q * rows : (q + 1) * rows]
                    shift = ((q - r) % PER) * feats
                    moved = piece if shift == 0 else pltpu.roll(piece, shift, 1)
                    packed = moved if packed is None else jnp.where(lanes >= q * feats, moved, packed)
                cs[g, r % 2, 2 * part + r // 2] = packed.astype(BF16)
            copy = remote(
                cs.at[g, 1 - c, pl.ds(2 * part, 2)], cr.at[g, pl.ds(2 * part, 2)],
                e_s.at[g, part], e_r.at[g, part], (partner, y, x),
            )
            copy.start()
            e_copies[g, part] = copy

    def stage_d(g):
        for part in range(wd.shape[0]):
            e_copies[g, part].wait_recv()
        for j in (4, 3, 5, 2, 6, 1, 7):
            to = lax.rem(z + j, n_z)
            zs[g, j] = (cs[g, c, to].astype(F32) + cr[g, to].astype(F32)).astype(BF16)
            copy = remote(zs.at[g, j], zr.at[g, j], f_s.at[g, j], f_r.at[g, j], dev_z(j))
            copy.start()
            f_copies[g, j] = copy

    def stage_e(g):
        total = cs[g, c, z].astype(F32) + cr[g, z].astype(F32)
        for j in (1, 7, 2, 6, 3, 5, 4):
            f_copies[g, j].wait_recv()
            total = total + zr[g, j].astype(F32)
        for q in reversed(range(PER)):
            k = g * PER + q
            moved = total if q == 0 else pltpu.roll(total, lane_group - q * feats, 1)
            block = moved[:, :128].astype(BF16)
            if k == 0:
                ret[0] = block
            else:
                ys[k] = block
                copy = remote(ys.at[k], ret.at[k], g_s.at[k], g_r.at[k], dev_y(OFFSETS[k]))
                copy.start()
                g_copies[k] = copy

    stage_a(0)
    stage_b(0)
    stage_c(0)
    stage_d(0)
    stage_a(1)
    stage_b(1)
    stage_c(1)
    stage_d(1)
    stage_e(0)
    stage_e(1)
    for k in range(1, SLOTS):
        g_copies[k].wait_recv()
    back = ret[...].reshape(SLOTS * rows, 128)
    dims = (((0,), (0,)), ((), ()))
    moe = lax.dot_general(pwh[...], back, dims, preferred_element_type=F32)
    moe = moe + lax.dot_general(pwl[...], back, dims, preferred_element_type=F32)
    out_ref[...] = moe
    for copy in a_copies[1:]:
        copy.wait_send()
    for group in (b_copies, c_copies, d_copies, e_copies, f_copies, g_copies):
        for copy in group.values():
            copy.wait_send()


def on_device(tokens, norm_gain, up_w, down_w, expert_ids, gate_gap):
    micro, _, row_count, width = tokens.shape
    n_tok = micro * row_count
    rows = micro * CAP
    units = up_w.shape[2]
    pipe = lax.axis_size("pipe")
    n_z = pipe // 2
    feats = width // pipe
    lane_group = PER * feats
    parts = width // lane_group
    flat = tokens.reshape(n_tok, width)
    ids = expert_ids[:, 0].reshape(n_tok, 2).T.astype(F32)
    gap = gate_gap[:, 0].reshape(1, n_tok)
    meta = jnp.concatenate([ids, gap], axis=0)
    vmem = pl.BlockSpec(memory_space=pltpu.VMEM)
    hbm = pl.BlockSpec(memory_space=pl.ANY)
    dma = pltpu.SemaphoreType.DMA
    moe = pl.pallas_call(
        layer_kernel,
        out_shape=jax.ShapeDtypeStruct((n_tok, 128), F32),
        in_specs=[vmem, vmem, vmem, hbm, hbm],
        out_specs=vmem,
        scratch_shapes=[
            pltpu.VMEM((width, units), BF16),
            pltpu.VMEM((parts, units, lane_group), BF16),
            pltpu.VMEM((SLOTS, rows, width // 2), BF16),
            pltpu.VMEM((2, SLOTS, rows, width // 2), BF16),
            pltpu.VMEM((GROUPS, PER * rows, width), BF16),
            pltpu.VMEM((GROUPS, PER, rows, units + 128), BF16),
            pltpu.VMEM((GROUPS, 4, rows, units + 128), BF16),
            pltpu.VMEM((GROUPS, PER, rows, units), BF16),
            pltpu.VMEM((GROUPS, 2, n_z, rows, lane_group), BF16),
            pltpu.VMEM((GROUPS, n_z, rows, lane_group), BF16),
            pltpu.VMEM((GROUPS, n_z, rows, lane_group), BF16),
            pltpu.VMEM((GROUPS, n_z, rows, lane_group), BF16),
            pltpu.VMEM((SLOTS, rows, 128), BF16),
            pltpu.VMEM((SLOTS, rows, 128), BF16),
            pltpu.VMEM((SLOTS * rows, n_tok), BF16),
            pltpu.VMEM((SLOTS * rows, n_tok), BF16),
            dma((1 + parts,)),
            dma((SLOTS,)), dma((SLOTS,)),
            dma((SLOTS,)), dma((SLOTS,)),
            dma((GROUPS, 4)), dma((GROUPS, 4)),
            dma((GROUPS, 4)), dma((GROUPS, 4)),
            dma((GROUPS, parts)), dma((GROUPS, parts)),
            dma((GROUPS, n_z)), dma((GROUPS, n_z)),
            dma((SLOTS,)), dma((SLOTS,)),
        ],
        compiler_params=pltpu.CompilerParams(
            collective_id=0, has_side_effects=True, vmem_limit_bytes=56 * 1024 * 1024
        ),
        name="expert_layer",
    )(flat, norm_gain.reshape(1, width), meta, up_w[0], down_w[0])
    start = lax.axis_index("pipe") * feats
    own = lax.dynamic_slice_in_dim(flat, start, feats, axis=1).astype(F32)
    result = (own + moe[:, :feats]).astype(BF16)
    return result.reshape(micro, 1, row_count, feats)


def solution(mesh):
    return jax.shard_map(
        on_device,
        mesh=mesh,
        in_specs=(
            P(None, "expert", None, "dp"),
            P("dp"),
            P("expert", "dp", "pipe"),
            P("expert", "pipe", "dp"),
            P(None, "expert", None, None),
            P(None, "expert", None),
        ),
        out_specs=P(None, "expert", None, ("dp", "pipe")),
        check_vma=False,
    )
```

```python
import jax
import jax.numpy as jnp
from jax import lax
from jax.experimental import pallas as pl
from jax.experimental.pallas import tpu as pltpu
from jax.sharding import PartitionSpec as P

MESH = pl.DeviceIdType.MESH
OFFSETS = (0, 1, -1, 2, -2, 3, -3, 4)
GROUPS = 2
SLOTS = 8
PER = 4
CAP = 6
F32 = jnp.float32
BF16 = jnp.bfloat16


def layer_kernel(
    tok_hbm, gain_ref, ids_ref, gap_ref, up_hbm, down_hbm, out_ref,
    tok_ref, wu, wd, pk, xg, xn, rs, rr, hb, cs, cr, zs, zr, ys, ret, pwh, pwl,
    w_sem, a_s, a_r, b_s, b_r, c_s, c_r, d_s, d_r, e_s, e_r, f_s, f_r, g_s, g_r,
):
    p = lax.axis_index("pipe")
    y = lax.axis_index("expert")
    x = lax.axis_index("dp")
    n_y = lax.axis_size("expert")
    n_x = lax.axis_size("dp")
    n_z = lax.axis_size("pipe") // 2
    z = p // 2
    c = p % 2
    partner = 2 * z + 1 - c
    n_tok, width = tok_ref.shape
    half = width // 2
    rows = n_tok // 16 * CAP
    row_half, lane_half = pk.shape[2:]
    units = wu.shape[1]
    feats = width // (2 * n_z)
    lane_group = PER * feats

    def dev_y(offset):
        return (p, lax.rem(y + offset + n_y, n_y), x)

    def dev_x(j):
        return (p, y, lax.rem(x + j, n_x))

    def dev_z(j):
        return (2 * lax.rem(z + j, n_z) + c, y, x)

    def remote(src, dst, s, r, dev):
        return pltpu.make_async_remote_copy(
            src_ref=src, dst_ref=dst, send_sem=s, recv_sem=r, device_id=dev, device_id_type=MESH
        )

    barrier = pltpu.get_barrier_semaphore()
    peers = [dev_y(o) for o in OFFSETS[1:]] + [dev_x(j) for j in range(1, 4)]
    peers += [dev_z(j) for j in range(1, 8)] + [(partner, y, x)]
    for dev in peers:
        pl.semaphore_signal(barrier, inc=1, device_id=dev, device_id_type=MESH)

    token_copy = pltpu.make_async_copy(tok_hbm, tok_ref, w_sem.at[0])
    token_copy.start()
    weight_copies = [pltpu.make_async_copy(up_hbm, wu, w_sem.at[1])]
    for part in range(wd.shape[0]):
        weight_copies.append(
            pltpu.make_async_copy(
                down_hbm.at[:, pl.ds(part * lane_group, lane_group)], wd.at[part], w_sem.at[2 + part]
            )
        )
    for copy in weight_copies:
        copy.start()

    sub = lax.broadcasted_iota(jnp.int32, (SLOTS, n_tok), 0)
    lane = lax.broadcasted_iota(jnp.int32, (SLOTS, n_tok), 1)
    offset = jnp.zeros_like(sub)
    for k in range(SLOTS):
        offset = jnp.where(sub == k, OFFSETS[k], offset)
    expert_of = y - offset
    expert_of = jnp.where(expert_of < 0, expert_of + n_y, expert_of)
    expert_of = jnp.where(expert_of >= n_y, expert_of - n_y, expert_of).astype(F32)
    spread = lax.broadcasted_iota(jnp.int32, (16, n_tok), 1) % 16
    spread = jnp.where(spread == lax.broadcasted_iota(jnp.int32, (16, n_tok), 0), 1.0, 0.0)

    def as_row(blocks):
        wide = jnp.dot(
            jnp.concatenate(blocks, axis=0), spread,
            preferred_element_type=F32, precision=lax.Precision.HIGHEST,
        )
        return jnp.sum(jnp.where(lane // 16 == sub, wide, 0.0), axis=0, keepdims=True)

    micros = range(n_tok // 16)
    first = as_row([ids_ref[m, 0, 0:1, :].astype(F32) for m in micros]) == expert_of
    second = as_row([ids_ref[m, 0, 1:2, :].astype(F32) for m in micros]) == expert_of
    share = 1.0 / (1.0 + jnp.exp(-as_row([gap_ref[m] for m in micros])))
    weight = jnp.where(first, share, 0.0) + jnp.where(second, 1.0 - share, 0.0)
    member = first | second
    before = lax.broadcasted_iota(jnp.int32, (n_tok, n_tok), 0)
    token = lax.broadcasted_iota(jnp.int32, (n_tok, n_tok), 1)
    block_of = (token // 16) == (before // 16)
    earlier = jnp.where(block_of & (before < token), 1.0, 0.0).astype(BF16)
    rank = jnp.dot(jnp.where(member, 1.0, 0.0).astype(BF16), earlier, preferred_element_type=F32)
    code = jnp.where(member, rank + ((lane // 16) * CAP).astype(F32), -1.0)
    row_id = lax.broadcasted_iota(jnp.int32, (rows, n_tok), 0).astype(F32)
    lo_half = pl.multiple_of(c * half, 128)
    token_copy.wait()
    own_half = tok_ref[:, pl.ds(lo_half, half)]
    gain = jnp.concatenate([gain_ref[i : i + 1, :] for i in range(width // 128)], axis=1)
    gains = [gain[:, i * lane_half : (i + 1) * lane_half] for i in range(width // lane_half)]
    for k in range(SLOTS):
        hit = code[k : k + 1, :] == row_id
        pick = jnp.where(hit, 1.0, 0.0).astype(BF16)
        if k == 0:
            value = jnp.dot(pick, tok_ref[...], preferred_element_type=F32).astype(BF16)
            for h in range(2):
                for w in range(4):
                    lo = h * half + (w % 2) * lane_half
                    xg[h, 0, w] = value[(w // 2) * row_half : (w // 2 + 1) * row_half, lo : lo + lane_half]
        else:
            value = jnp.dot(pick, own_half, preferred_element_type=F32).astype(BF16)
            for w in range(4):
                lo = (w % 2) * lane_half
                pk[k, w] = value[(w // 2) * row_half : (w // 2 + 1) * row_half, lo : lo + lane_half]

    pl.semaphore_wait(barrier, len(peers))

    quarter = z % 4
    a_copies, h_copies, b_copies = {}, {}, {}
    for k in (1, 2):
        a_copies[k] = remote(pk.at[k], xg.at[c, k], a_s.at[k, 0], a_r.at[k, 0], dev_y(-OFFSETS[k]))
        a_copies[k].start()
    for k in (7, 5, 6, 3, 4):
        a_copies[k] = remote(
            pk.at[k, quarter], xg.at[c, k, quarter], a_s.at[k, 0], a_r.at[k, 0], dev_y(-OFFSETS[k])
        )
        a_copies[k].start()

    for k in range(SLOTS):
        hit = code[k : k + 1, :] == row_id
        placed = jnp.where(hit, weight[k : k + 1, :], 0.0)
        high = placed.astype(BF16)
        pwh[pl.ds(k * rows, rows), :] = high
        pwl[pl.ds(k * rows, rows), :] = (placed - high.astype(F32)).astype(BF16)

    c_copies, d_copies, e_copies, f_copies, g_copies = {}, {}, {}, {}, {}

    def share_far(k):
        a_copies[k].wait_recv()
        block = xg.at[c, k, quarter]
        two_away = 2 * lax.rem(z + 2 + 4 * c, n_z) + c
        for i, dev in ((1, dev_z(1)), (2, dev_z(7)), (3, (two_away, y, x))):
            copy = remote(block, block, a_s.at[k, i], a_r.at[k, i], dev)
            copy.start()
            h_copies[k, i] = copy

    def to_partner(k):
        if k > 2:
            for i in (1, 2, 3):
                h_copies[k, i].wait_recv()
        else:
            a_copies[k].wait_recv()
        b_copies[k] = remote(xg.at[c, k], xg.at[c, k], b_s.at[k], b_r.at[k], (partner, y, x))
        b_copies[k].start()

    totals = {}

    def prepare(k, h, own):
        g, q = k // PER, k % PER
        for rh in range(2):
            total = totals.get((k, rh), jnp.zeros((row_half, 1), F32))
            for lh in range(2):
                block = xg[h, k, 2 * rh + lh].astype(F32)
                total = total + jnp.sum(block * block, axis=-1, keepdims=True)
                if isinstance(h, int):
                    factor, lo = gains[2 * h + lh], h * half + lh * lane_half
                else:
                    factor = jnp.where(h == 0, gains[lh], gains[2 + lh])
                    lo = pl.multiple_of(h * half + lh * lane_half, 128)
                xn[g, pl.ds(q * rows + rh * row_half, row_half), pl.ds(lo, lane_half)] = (
                    block * factor
                ).astype(BF16)
            totals[k, rh] = total

    def prepare_other(k):
        b_copies[k].wait_recv()
        prepare(k, 1 - c, False)

    def stage_a(g):
        if g == 0:
            weight_copies[0].wait()
        gate = jnp.dot(xn[g], wu[...], preferred_element_type=F32)
        lanes = lax.broadcasted_iota(jnp.int32, (rows, 128), 1)
        for q in range(PER):
            rs[g, q, :, pl.ds(0, units)] = gate[q * rows : (q + 1) * rows].astype(BF16)
            both = [jnp.broadcast_to(totals[g * PER + q, rh], (row_half, 128)) for rh in range(2)]
            square = jnp.concatenate(both, axis=0)
            high = square.astype(BF16).astype(F32)
            rs[g, q, :, pl.ds(units, 128)] = jnp.where(lanes < 64, high, square - high).astype(BF16)
        for j in range(1, 4):
            copy = remote(rs.at[g, lax.rem(x + j, n_x)], rr.at[g, j], c_s.at[g, j], c_r.at[g, j], dev_x(j))
            copy.start()
            c_copies[g, j] = copy

    def stage_b(g):
        total = rs[g, x].astype(F32)
        for j in range(1, 4):
            c_copies[g, j].wait_recv()
            total = total + rr[g, j].astype(F32)
        square = total[:, units : units + 1] + total[:, units + 64 : units + 65]
        scale = lax.rsqrt(square / (width * n_x) + 1e-05)
        gate = total[:, :units] * scale
        hb[g, x] = (gate / (1.0 + jnp.exp(-gate))).astype(BF16)
        for j in range(1, 4):
            copy = remote(hb.at[g, x], hb.at[g, x], d_s.at[g, j], d_r.at[g, j], dev_x(j))
            copy.start()
            d_copies[g, j] = copy

    def stage_c(g):
        for j in range(1, 4):
            d_copies[g, j].wait_recv()
        hidden = hb[g].reshape(PER * rows, units)
        if g == 0:
            for copy in weight_copies[1:]:
                copy.wait()
        lanes = lax.broadcasted_iota(jnp.int32, (rows, lane_group), 1)
        for part in range(wd.shape[0]):
            outs = jnp.dot(hidden, wd[part], preferred_element_type=F32)
            for r in range(PER):
                packed = None
                for q in range(PER):
                    piece = outs[q * rows : (q + 1) * rows]
                    shift = ((q - r) % PER) * feats
                    moved = piece if shift == 0 else pltpu.roll(piece, shift, 1)
                    packed = moved if packed is None else jnp.where(lanes >= q * feats, moved, packed)
                cs[g, r % 2, 2 * part + r // 2] = packed.astype(BF16)
            copy = remote(
                cs.at[g, 1 - c, pl.ds(2 * part, 2)], cr.at[g, pl.ds(2 * part, 2)],
                e_s.at[g, part], e_r.at[g, part], (partner, y, x),
            )
            copy.start()
            e_copies[g, part] = copy

    def stage_d(g):
        for part in range(wd.shape[0]):
            e_copies[g, part].wait_recv()
        for j in (4, 3, 5, 2, 6, 1, 7):
            to = lax.rem(z + j, n_z)
            zs[g, j] = (cs[g, c, to].astype(F32) + cr[g, to].astype(F32)).astype(BF16)
            copy = remote(zs.at[g, j], zr.at[g, j], f_s.at[g, j], f_r.at[g, j], dev_z(j))
            copy.start()
            f_copies[g, j] = copy

    def stage_e(g):
        total = cs[g, c, z].astype(F32) + cr[g, z].astype(F32)
        for j in (1, 7, 2, 6, 3, 5, 4):
            f_copies[g, j].wait_recv()
            total = total + zr[g, j].astype(F32)
        for q in reversed(range(PER)):
            k = g * PER + q
            moved = total if q == 0 else pltpu.roll(total, lane_group - q * feats, 1)
            block = moved[:, :128].astype(BF16)
            if k == 0:
                ret[0] = block
            else:
                ys[k] = block
                copy = remote(ys.at[k], ret.at[k], g_s.at[k], g_r.at[k], dev_y(OFFSETS[k]))
                copy.start()
                g_copies[k] = copy

    prepare(0, 0, True)
    prepare(0, 1, True)
    to_partner(1)
    to_partner(2)
    prepare(1, c, True)
    prepare(2, c, True)
    share_far(3)
    share_far(4)
    prepare_other(1)
    prepare_other(2)
    share_far(5)
    share_far(6)
    to_partner(3)
    share_far(7)
    prepare(3, c, True)
    prepare_other(3)
    stage_a(0)
    for k in range(PER, SLOTS):
        to_partner(k)
        prepare(k, c, True)
    for k in range(PER, SLOTS):
        prepare_other(k)
    stage_a(1)
    stage_b(0)
    stage_b(1)
    stage_c(0)
    stage_d(0)
    stage_c(1)
    stage_d(1)
    stage_e(0)
    stage_e(1)
    for k in range(1, SLOTS):
        g_copies[k].wait_recv()
    back = ret[...].reshape(SLOTS * rows, 128)
    dims = (((0,), (0,)), ((), ()))
    moe = lax.dot_general(pwh[...], back, dims, preferred_element_type=F32)
    moe = moe + lax.dot_general(pwl[...], back, dims, preferred_element_type=F32)
    out_ref[...] = moe
    for group in (a_copies, h_copies, b_copies, c_copies, d_copies, e_copies, f_copies, g_copies):
        for copy in group.values():
            copy.wait_send()


def on_device(tokens, norm_gain, up_w, down_w, expert_ids, gate_gap):
    micro, _, row_count, width = tokens.shape
    n_tok = micro * row_count
    rows = micro * CAP
    units = up_w.shape[2]
    pipe = lax.axis_size("pipe")
    n_z = pipe // 2
    feats = width // pipe
    lane_group = PER * feats
    parts = width // lane_group
    flat = tokens.reshape(n_tok, width)
    ids = expert_ids.transpose(0, 1, 3, 2)
    vmem = pl.BlockSpec(memory_space=pltpu.VMEM)
    hbm = pl.BlockSpec(memory_space=pl.ANY)
    dma = pltpu.SemaphoreType.DMA
    moe = pl.pallas_call(
        layer_kernel,
        out_shape=jax.ShapeDtypeStruct((n_tok, 128), F32),
        in_specs=[hbm, vmem, vmem, vmem, hbm, hbm],
        out_specs=vmem,
        scratch_shapes=[
            pltpu.VMEM((n_tok, width), BF16),
            pltpu.VMEM((width, units), BF16),
            pltpu.VMEM((parts, units, lane_group), BF16),
            pltpu.VMEM((SLOTS, 4, rows // 2, width // 4), BF16),
            pltpu.VMEM((2, SLOTS, 4, rows // 2, width // 4), BF16),
            pltpu.VMEM((GROUPS, PER * rows, width), BF16),
            pltpu.VMEM((GROUPS, PER, rows, units + 128), BF16),
            pltpu.VMEM((GROUPS, 4, rows, units + 128), BF16),
            pltpu.VMEM((GROUPS, PER, rows, units), BF16),
            pltpu.VMEM((GROUPS, 2, n_z, rows, lane_group), BF16),
            pltpu.VMEM((GROUPS, n_z, rows, lane_group), BF16),
            pltpu.VMEM((GROUPS, n_z, rows, lane_group), BF16),
            pltpu.VMEM((GROUPS, n_z, rows, lane_group), BF16),
            pltpu.VMEM((SLOTS, rows, 128), BF16),
            pltpu.VMEM((SLOTS, rows, 128), BF16),
            pltpu.VMEM((SLOTS * rows, n_tok), BF16),
            pltpu.VMEM((SLOTS * rows, n_tok), BF16),
            dma((2 + parts,)),
            dma((SLOTS, 4)), dma((SLOTS, 4)),
            dma((SLOTS,)), dma((SLOTS,)),
            dma((GROUPS, 4)), dma((GROUPS, 4)),
            dma((GROUPS, 4)), dma((GROUPS, 4)),
            dma((GROUPS, parts)), dma((GROUPS, parts)),
            dma((GROUPS, n_z)), dma((GROUPS, n_z)),
            dma((SLOTS,)), dma((SLOTS,)),
        ],
        compiler_params=pltpu.CompilerParams(
            collective_id=0, has_side_effects=True, vmem_limit_bytes=56 * 1024 * 1024
        ),
        name="expert_layer",
    )(flat, norm_gain.reshape(width // 128, 128), ids, gate_gap, up_w[0], down_w[0])
    start = lax.axis_index("pipe") * feats
    own = lax.dynamic_slice_in_dim(flat, start, feats, axis=1).astype(F32)
    result = (own + moe[:, :feats]).astype(BF16)
    return result.reshape(micro, 1, row_count, feats)


def solution(mesh):
    return jax.shard_map(
        on_device,
        mesh=mesh,
        in_specs=(
            P(None, "expert", None, "dp"),
            P("dp"),
            P("expert", "dp", "pipe"),
            P("expert", "pipe", "dp"),
            P(None, "expert", None, None),
            P(None, "expert", None),
        ),
        out_specs=P(None, "expert", None, ("dp", "pipe")),
        check_vma=False,
    )
```

```python
import jax
import jax.numpy as jnp
from jax import lax
from jax.experimental import pallas as pl
from jax.experimental.pallas import tpu as pltpu
from jax.sharding import PartitionSpec as P

MESH = pl.DeviceIdType.MESH
OFFSETS = (0, 1, -1, 2, -2, 3, -3, 4)
SLOTS = 8
PER = 2
GROUPS = SLOTS // PER
CAP = 6
F32 = jnp.float32
BF16 = jnp.bfloat16


def layer_kernel(
    tok_hbm, gain_ref, ids_ref, gap_ref, up_hbm, down_hbm, out_ref,
    tok_ref, wu, wd, pk, xg, xn, rs, rr, hb, cs, cr, zs, zr, ys, ret, pwh, pwl,
    w_sem, a_s, a_r, b_s, b_r, c_s, c_r, d_s, d_r, e_s, e_r, f_s, f_r, g_s, g_r,
):
    p = lax.axis_index("pipe")
    y = lax.axis_index("expert")
    x = lax.axis_index("dp")
    n_y = lax.axis_size("expert")
    n_x = lax.axis_size("dp")
    n_z = lax.axis_size("pipe") // 2
    z = p // 2
    c = p % 2
    partner = 2 * z + 1 - c
    n_tok, width = tok_ref.shape
    half = width // 2
    rows = n_tok // 16 * CAP
    row_half, lane_half = pk.shape[2:]
    units = wu.shape[1]
    feats = width // (2 * n_z)
    lane_group = 4 * feats
    piece_rows = PER * rows // 4

    def dev_y(offset):
        return (p, lax.rem(y + offset + n_y, n_y), x)

    def dev_x(j):
        return (p, y, lax.rem(x + j, n_x))

    def dev_z(j):
        return (2 * lax.rem(z + j, n_z) + c, y, x)

    def remote(src, dst, s, r, dev):
        return pltpu.make_async_remote_copy(
            src_ref=src, dst_ref=dst, send_sem=s, recv_sem=r, device_id=dev, device_id_type=MESH
        )

    barrier = pltpu.get_barrier_semaphore()
    peers = [dev_y(o) for o in OFFSETS[1:]] + [dev_x(j) for j in range(1, 4)]
    peers += [dev_z(j) for j in range(1, 8)] + [(partner, y, x)]
    for dev in peers:
        pl.semaphore_signal(barrier, inc=1, device_id=dev, device_id_type=MESH)

    token_copy = pltpu.make_async_copy(tok_hbm, tok_ref, w_sem.at[0])
    token_copy.start()
    weight_copies = [pltpu.make_async_copy(up_hbm, wu, w_sem.at[1])]
    for part in range(wd.shape[0]):
        weight_copies.append(
            pltpu.make_async_copy(
                down_hbm.at[:, pl.ds(part * lane_group, lane_group)], wd.at[part], w_sem.at[2 + part]
            )
        )
    for copy in weight_copies:
        copy.start()

    sub = lax.broadcasted_iota(jnp.int32, (SLOTS, n_tok), 0)
    lane = lax.broadcasted_iota(jnp.int32, (SLOTS, n_tok), 1)
    offset = jnp.zeros_like(sub)
    for k in range(SLOTS):
        offset = jnp.where(sub == k, OFFSETS[k], offset)
    expert_of = y - offset
    expert_of = jnp.where(expert_of < 0, expert_of + n_y, expert_of)
    expert_of = jnp.where(expert_of >= n_y, expert_of - n_y, expert_of).astype(F32)
    spread = lax.broadcasted_iota(jnp.int32, (16, n_tok), 1) % 16
    spread = jnp.where(spread == lax.broadcasted_iota(jnp.int32, (16, n_tok), 0), 1.0, 0.0)

    def as_row(blocks):
        wide = jnp.dot(
            jnp.concatenate(blocks, axis=0), spread,
            preferred_element_type=F32, precision=lax.Precision.HIGHEST,
        )
        return jnp.sum(jnp.where(lane // 16 == sub, wide, 0.0), axis=0, keepdims=True)

    micros = range(n_tok // 16)
    first = as_row([ids_ref[m, 0, 0:1, :].astype(F32) for m in micros]) == expert_of
    second = as_row([ids_ref[m, 0, 1:2, :].astype(F32) for m in micros]) == expert_of
    share = 1.0 / (1.0 + jnp.exp(-as_row([gap_ref[m] for m in micros])))
    weight = jnp.where(first, share, 0.0) + jnp.where(second, 1.0 - share, 0.0)
    member = first | second
    before = lax.broadcasted_iota(jnp.int32, (n_tok, n_tok), 0)
    token = lax.broadcasted_iota(jnp.int32, (n_tok, n_tok), 1)
    block_of = (token // 16) == (before // 16)
    earlier = jnp.where(block_of & (before < token), 1.0, 0.0).astype(BF16)
    rank = jnp.dot(jnp.where(member, 1.0, 0.0).astype(BF16), earlier, preferred_element_type=F32)
    code = jnp.where(member, rank + ((lane // 16) * CAP).astype(F32), -1.0)
    row_id = lax.broadcasted_iota(jnp.int32, (rows, n_tok), 0).astype(F32)
    lo_half = pl.multiple_of(c * half, 128)
    token_copy.wait()
    own_half = tok_ref[:, pl.ds(lo_half, half)]
    gain = jnp.concatenate([gain_ref[i : i + 1, :] for i in range(width // 128)], axis=1)
    gains = [gain[:, i * lane_half : (i + 1) * lane_half] for i in range(width // lane_half)]
    for k in range(SLOTS):
        hit = code[k : k + 1, :] == row_id
        pick = jnp.where(hit, 1.0, 0.0).astype(BF16)
        if k == 0:
            value = jnp.dot(pick, tok_ref[...], preferred_element_type=F32).astype(BF16)
            for h in range(2):
                for w in range(4):
                    lo = h * half + (w % 2) * lane_half
                    xg[h, 0, w] = value[(w // 2) * row_half : (w // 2 + 1) * row_half, lo : lo + lane_half]
        else:
            value = jnp.dot(pick, own_half, preferred_element_type=F32).astype(BF16)
            for w in range(4):
                lo = (w % 2) * lane_half
                pk[k, w] = value[(w // 2) * row_half : (w // 2 + 1) * row_half, lo : lo + lane_half]

    pl.semaphore_wait(barrier, len(peers))

    quarter = z % 4
    a_copies, h_copies, b_copies = {}, {}, {}
    for k in (1, 2):
        a_copies[k] = remote(pk.at[k], xg.at[c, k], a_s.at[k, 0], a_r.at[k, 0], dev_y(-OFFSETS[k]))
        a_copies[k].start()
    for k in (7, 5, 6, 3, 4):
        a_copies[k] = remote(
            pk.at[k, quarter], xg.at[c, k, quarter], a_s.at[k, 0], a_r.at[k, 0], dev_y(-OFFSETS[k])
        )
        a_copies[k].start()

    for k in range(SLOTS):
        hit = code[k : k + 1, :] == row_id
        placed = jnp.where(hit, weight[k : k + 1, :], 0.0)
        high = placed.astype(BF16)
        pwh[pl.ds(k * rows, rows), :] = high
        pwl[pl.ds(k * rows, rows), :] = (placed - high.astype(F32)).astype(BF16)

    c_copies, d_copies, e_copies, f_copies, g_copies = {}, {}, {}, {}, {}

    def share_far(k):
        a_copies[k].wait_recv()
        block = xg.at[c, k, quarter]
        two_away = 2 * lax.rem(z + 2 + 4 * c, n_z) + c
        for i, dev in ((1, dev_z(1)), (2, dev_z(7)), (3, (two_away, y, x))):
            copy = remote(block, block, a_s.at[k, i], a_r.at[k, i], dev)
            copy.start()
            h_copies[k, i] = copy

    def to_partner(k):
        if k > 2:
            for i in (1, 2, 3):
                h_copies[k, i].wait_recv()
        else:
            a_copies[k].wait_recv()
        b_copies[k] = remote(xg.at[c, k], xg.at[c, k], b_s.at[k], b_r.at[k], (partner, y, x))
        b_copies[k].start()

    totals = {}

    def prepare(k, h, own):
        g, q = k // PER, k % PER
        for rh in range(2):
            total = totals.get((k, rh), jnp.zeros((row_half, 1), F32))
            for lh in range(2):
                block = xg[h, k, 2 * rh + lh].astype(F32)
                total = total + jnp.sum(block * block, axis=-1, keepdims=True)
                if isinstance(h, int):
                    factor, lo = gains[2 * h + lh], h * half + lh * lane_half
                else:
                    factor = jnp.where(h == 0, gains[lh], gains[2 + lh])
                    lo = pl.multiple_of(h * half + lh * lane_half, 128)
                xn[g, pl.ds(q * rows + rh * row_half, row_half), pl.ds(lo, lane_half)] = (
                    block * factor
                ).astype(BF16)
            totals[k, rh] = total

    def prepare_other(k):
        b_copies[k].wait_recv()
        prepare(k, 1 - c, False)

    def stage_a(g):
        if g == 0:
            weight_copies[0].wait()
        gate = jnp.dot(xn[g], wu[...], preferred_element_type=F32)
        lanes = lax.broadcasted_iota(jnp.int32, (PER * rows, 128), 1)
        square = jnp.concatenate(
            [
                jnp.broadcast_to(totals[k, rh], (row_half, 128))
                for k in range(g * PER, (g + 1) * PER) for rh in range(2)
            ],
            axis=0,
        )
        high = square.astype(BF16).astype(F32)
        square = jnp.where(lanes < 64, high, square - high).astype(BF16)
        gate = gate.astype(BF16)
        for q in range(4):
            rs[g, q, :, pl.ds(0, units)] = gate[q * piece_rows : (q + 1) * piece_rows]
            rs[g, q, :, pl.ds(units, 128)] = square[q * piece_rows : (q + 1) * piece_rows]
        for j in range(1, 4):
            copy = remote(rs.at[g, lax.rem(x + j, n_x)], rr.at[g, j], c_s.at[g, j], c_r.at[g, j], dev_x(j))
            copy.start()
            c_copies[g, j] = copy

    def stage_b(g):
        total = rs[g, x].astype(F32)
        for j in range(1, 4):
            c_copies[g, j].wait_recv()
            total = total + rr[g, j].astype(F32)
        square = total[:, units : units + 1] + total[:, units + 64 : units + 65]
        scale = lax.rsqrt(square / (width * n_x) + 1e-05)
        gate = total[:, :units] * scale
        hb[g, x] = (gate / (1.0 + jnp.exp(-gate))).astype(BF16)
        for j in range(1, 4):
            copy = remote(hb.at[g, x], hb.at[g, x], d_s.at[g, j], d_r.at[g, j], dev_x(j))
            copy.start()
            d_copies[g, j] = copy

    def stage_c(g):
        for j in range(1, 4):
            d_copies[g, j].wait_recv()
        hidden = hb[g].reshape(4 * piece_rows, units)
        if g == 0:
            for copy in weight_copies[1:]:
                copy.wait()
        lanes = lax.broadcasted_iota(jnp.int32, (piece_rows, lane_group), 1)
        for part in range(wd.shape[0]):
            outs = jnp.dot(hidden, wd[part], preferred_element_type=F32)
            for r in range(4):
                packed = None
                for q in range(4):
                    piece = outs[q * piece_rows : (q + 1) * piece_rows]
                    shift = ((q - r) % 4) * feats
                    moved = piece if shift == 0 else pltpu.roll(piece, shift, 1)
                    packed = moved if packed is None else jnp.where(lanes >= q * feats, moved, packed)
                cs[g, r % 2, 2 * part + r // 2] = packed.astype(BF16)
            copy = remote(
                cs.at[g, 1 - c, pl.ds(2 * part, 2)], cr.at[g, pl.ds(2 * part, 2)],
                e_s.at[g, part], e_r.at[g, part], (partner, y, x),
            )
            copy.start()
            e_copies[g, part] = copy

    def stage_d(g):
        for part in range(wd.shape[0]):
            e_copies[g, part].wait_recv()
        for j in (4, 3, 5, 2, 6, 1, 7):
            to = lax.rem(z + j, n_z)
            zs[g, j] = (cs[g, c, to].astype(F32) + cr[g, to].astype(F32)).astype(BF16)
            copy = remote(zs.at[g, j], zr.at[g, j], f_s.at[g, j], f_r.at[g, j], dev_z(j))
            copy.start()
            f_copies[g, j] = copy

    def stage_e(g):
        total = cs[g, c, z].astype(F32) + cr[g, z].astype(F32)
        for j in (1, 7, 2, 6, 3, 5, 4):
            f_copies[g, j].wait_recv()
            total = total + zr[g, j].astype(F32)
        for k in range(g * PER, (g + 1) * PER):
            for i in range(4 // PER):
                q = (k % PER) * (4 // PER) + i
                moved = total if q == 0 else pltpu.roll(total, lane_group - q * feats, 1)
                block = moved[:, :128].astype(BF16)
                if k == 0:
                    ret[k, pl.ds(i * piece_rows, piece_rows)] = block
                else:
                    ys[k, pl.ds(i * piece_rows, piece_rows)] = block
            if k > 0:
                copy = remote(ys.at[k], ret.at[k], g_s.at[k], g_r.at[k], dev_y(OFFSETS[k]))
                copy.start()
                g_copies[k] = copy

    prepare(0, 0, True)
    prepare(0, 1, True)
    to_partner(1)
    to_partner(2)
    prepare(1, c, True)
    share_far(3)
    share_far(4)
    prepare_other(1)
    stage_a(0)
    share_far(5)
    share_far(6)
    share_far(7)
    prepare(2, c, True)
    prepare_other(2)
    to_partner(3)
    prepare(3, c, True)
    to_partner(4)
    prepare_other(3)
    stage_a(1)
    to_partner(5)
    prepare(4, c, True)
    prepare(5, c, True)
    prepare_other(4)
    to_partner(6)
    to_partner(7)
    stage_b(0)
    prepare_other(5)
    stage_a(2)
    prepare(6, c, True)
    prepare(7, c, True)
    stage_b(1)
    stage_c(0)
    prepare_other(6)
    prepare_other(7)
    stage_a(3)
    stage_d(0)
    stage_b(2)
    stage_c(1)
    stage_d(1)
    stage_b(3)
    stage_c(2)
    stage_d(2)
    stage_c(3)
    stage_d(3)
    stage_e(0)
    stage_e(1)
    stage_e(2)
    stage_e(3)
    for k in range(1, SLOTS):
        g_copies[k].wait_recv()
    back = ret[...].reshape(SLOTS * rows, 128)
    dims = (((0,), (0,)), ((), ()))
    moe = lax.dot_general(pwh[...], back, dims, preferred_element_type=F32)
    moe = moe + lax.dot_general(pwl[...], back, dims, preferred_element_type=F32)
    out_ref[...] = moe
    for group in (a_copies, h_copies, b_copies, c_copies, d_copies, e_copies, f_copies, g_copies):
        for copy in group.values():
            copy.wait_send()


def on_device(tokens, norm_gain, up_w, down_w, expert_ids, gate_gap):
    micro, _, row_count, width = tokens.shape
    n_tok = micro * row_count
    rows = micro * CAP
    units = up_w.shape[2]
    pipe = lax.axis_size("pipe")
    n_z = pipe // 2
    feats = width // pipe
    lane_group = 4 * feats
    piece_rows = PER * rows // 4
    parts = width // lane_group
    flat = tokens.reshape(n_tok, width)
    ids = expert_ids.transpose(0, 1, 3, 2)
    vmem = pl.BlockSpec(memory_space=pltpu.VMEM)
    hbm = pl.BlockSpec(memory_space=pl.ANY)
    dma = pltpu.SemaphoreType.DMA
    moe = pl.pallas_call(
        layer_kernel,
        out_shape=jax.ShapeDtypeStruct((n_tok, 128), F32),
        in_specs=[hbm, vmem, vmem, vmem, hbm, hbm],
        out_specs=vmem,
        scratch_shapes=[
            pltpu.VMEM((n_tok, width), BF16),
            pltpu.VMEM((width, units), BF16),
            pltpu.VMEM((parts, units, lane_group), BF16),
            pltpu.VMEM((SLOTS, 4, rows // 2, width // 4), BF16),
            pltpu.VMEM((2, SLOTS, 4, rows // 2, width // 4), BF16),
            pltpu.VMEM((GROUPS, PER * rows, width), BF16),
            pltpu.VMEM((GROUPS, 4, piece_rows, units + 128), BF16),
            pltpu.VMEM((GROUPS, 4, piece_rows, units + 128), BF16),
            pltpu.VMEM((GROUPS, 4, piece_rows, units), BF16),
            pltpu.VMEM((GROUPS, 2, n_z, piece_rows, lane_group), BF16),
            pltpu.VMEM((GROUPS, n_z, piece_rows, lane_group), BF16),
            pltpu.VMEM((GROUPS, n_z, piece_rows, lane_group), BF16),
            pltpu.VMEM((GROUPS, n_z, piece_rows, lane_group), BF16),
            pltpu.VMEM((SLOTS, rows, 128), BF16),
            pltpu.VMEM((SLOTS, rows, 128), BF16),
            pltpu.VMEM((SLOTS * rows, n_tok), BF16),
            pltpu.VMEM((SLOTS * rows, n_tok), BF16),
            dma((2 + parts,)),
            dma((SLOTS, 4)), dma((SLOTS, 4)),
            dma((SLOTS,)), dma((SLOTS,)),
            dma((GROUPS, 4)), dma((GROUPS, 4)),
            dma((GROUPS, 4)), dma((GROUPS, 4)),
            dma((GROUPS, parts)), dma((GROUPS, parts)),
            dma((GROUPS, n_z)), dma((GROUPS, n_z)),
            dma((SLOTS,)), dma((SLOTS,)),
        ],
        compiler_params=pltpu.CompilerParams(
            collective_id=0, has_side_effects=True, vmem_limit_bytes=56 * 1024 * 1024
        ),
        name="expert_layer",
    )(flat, norm_gain.reshape(width // 128, 128), ids, gate_gap, up_w[0], down_w[0])
    start = lax.axis_index("pipe") * feats
    own = lax.dynamic_slice_in_dim(flat, start, feats, axis=1).astype(F32)
    result = (own + moe[:, :feats]).astype(BF16)
    return result.reshape(micro, 1, row_count, feats)


def solution(mesh):
    return jax.shard_map(
        on_device,
        mesh=mesh,
        in_specs=(
            P(None, "expert", None, "dp"),
            P("dp"),
            P("expert", "dp", "pipe"),
            P("expert", "pipe", "dp"),
            P(None, "expert", None, None),
            P(None, "expert", None),
        ),
        out_specs=P(None, "expert", None, ("dp", "pipe")),
        check_vma=False,
    )
```

```python
import jax
import jax.numpy as jnp
from jax import lax
from jax.experimental import pallas as pl
from jax.experimental.pallas import tpu as pltpu
from jax.sharding import PartitionSpec as P

MESH = pl.DeviceIdType.MESH
OFFSETS = (0, 1, -1, 2, -2, 3, -3, 4)
SLOTS = 8
PER = 2
GROUPS = SLOTS // PER
NEAR = (1, 2)
FAR = (7, 5, 6, 3, 4)
RELAYED = (0, 3, 2)
CAP = 6
F32 = jnp.float32
BF16 = jnp.bfloat16


def layer_kernel(
    tok_hbm, gain_hbm, ids_hbm, gap_hbm, up_hbm, down_hbm, out_ref,
    tok_ref, own_ref, gain_ref, ids_ref, gap_ref, wu, wd, pk, xg, xn, rs, rr, hb, cs, cr, zs, zr, ys, ret, pwh, pwl,
    w_sem, a_s, a_r, b_s, b_r, c_s, c_r, d_s, d_r, e_s, e_r, f_s, f_r, g_s, g_r,
):
    p = lax.axis_index("pipe")
    y = lax.axis_index("expert")
    x = lax.axis_index("dp")
    n_y = lax.axis_size("expert")
    n_x = lax.axis_size("dp")
    n_z = lax.axis_size("pipe") // 2
    z = p // 2
    c = p % 2
    partner = 2 * z + 1 - c
    n_tok, width = tok_ref.shape
    half = width // 2
    rows = n_tok // 16 * CAP
    row_half, lane_half = pk.shape[2:]
    units = wu.shape[1]
    feats = width // (2 * n_z)
    lane_group = 4 * feats
    piece_rows = PER * rows // 4

    def dev_y(offset):
        return (p, lax.rem(y + offset + n_y, n_y), x)

    def dev_x(j):
        return (p, y, lax.rem(x + j, n_x))

    def dev_z(j):
        return (2 * lax.rem(z + j, n_z) + c, y, x)

    def remote(src, dst, s, r, dev):
        return pltpu.make_async_remote_copy(
            src_ref=src, dst_ref=dst, send_sem=s, recv_sem=r, device_id=dev, device_id_type=MESH
        )

    barrier = pltpu.get_barrier_semaphore()
    peers = [dev_y(o) for o in OFFSETS[1:]] + [dev_x(j) for j in range(1, 4)]
    peers += [dev_z(j) for j in range(1, 8)] + [(partner, y, x)]
    for dev in peers:
        pl.semaphore_signal(barrier, inc=1, device_id=dev, device_id_type=MESH)

    small_copies = [
        pltpu.make_async_copy(src, dst, w_sem.at[i])
        for i, (src, dst) in enumerate(((ids_hbm, ids_ref), (gap_hbm, gap_ref), (gain_hbm, gain_ref)))
    ]
    token_copy = pltpu.make_async_copy(tok_hbm, tok_ref, w_sem.at[3])
    for copy in small_copies:
        copy.start()
    token_copy.start()
    weight_copies = [pltpu.make_async_copy(up_hbm, wu, w_sem.at[4])]
    for part in range(wd.shape[0]):
        weight_copies.append(
            pltpu.make_async_copy(
                down_hbm.at[:, pl.ds(part * lane_group, lane_group)], wd.at[part], w_sem.at[5 + part]
            )
        )
    for copy in weight_copies:
        copy.start()

    sub = lax.broadcasted_iota(jnp.int32, (SLOTS, n_tok), 0)
    lane = lax.broadcasted_iota(jnp.int32, (SLOTS, n_tok), 1)
    offset = jnp.zeros_like(sub)
    for k in range(SLOTS):
        offset = jnp.where(sub == k, OFFSETS[k], offset)
    expert_of = y - offset
    expert_of = jnp.where(expert_of < 0, expert_of + n_y, expert_of)
    expert_of = jnp.where(expert_of >= n_y, expert_of - n_y, expert_of).astype(F32)
    spread = lax.broadcasted_iota(jnp.int32, (16, n_tok), 1) % 16
    spread = jnp.where(spread == lax.broadcasted_iota(jnp.int32, (16, n_tok), 0), 1.0, 0.0)

    def as_row(blocks):
        wide = jnp.dot(
            jnp.concatenate(blocks, axis=0), spread,
            preferred_element_type=F32, precision=lax.Precision.HIGHEST,
        )
        return jnp.sum(jnp.where(lane // 16 == sub, wide, 0.0), axis=0, keepdims=True)

    micros = range(n_tok // 16)
    for copy in small_copies:
        copy.wait()
    first = as_row([ids_ref[m, 0, 0:1, :].astype(F32) for m in micros]) == expert_of
    second = as_row([ids_ref[m, 0, 1:2, :].astype(F32) for m in micros]) == expert_of
    share = 1.0 / (1.0 + jnp.exp(-as_row([gap_ref[m] for m in micros])))
    weight = jnp.where(first, share, 0.0) + jnp.where(second, 1.0 - share, 0.0)
    member = first | second
    before = lax.broadcasted_iota(jnp.int32, (n_tok, n_tok), 0)
    token = lax.broadcasted_iota(jnp.int32, (n_tok, n_tok), 1)
    block_of = (token // 16) == (before // 16)
    earlier = jnp.where(block_of & (before < token), 1.0, 0.0).astype(BF16)
    rank = jnp.dot(jnp.where(member, 1.0, 0.0).astype(BF16), earlier, preferred_element_type=F32)
    code = jnp.where(member, rank + ((lane // 16) * CAP).astype(F32), -1.0)
    row_id = lax.broadcasted_iota(jnp.int32, (rows, n_tok), 0).astype(F32)
    lo_half = pl.multiple_of(c * half, 128)
    token_copy.wait()
    own_half = tok_ref[:, pl.ds(lo_half, half)]
    gain = jnp.concatenate([gain_ref[i : i + 1, :] for i in range(width // 128)], axis=1)
    gains = [gain[:, i * lane_half : (i + 1) * lane_half] for i in range(width // lane_half)]
    for k in range(SLOTS):
        hit = code[k : k + 1, :] == row_id
        pick = jnp.where(hit, 1.0, 0.0).astype(BF16)
        if k == 0:
            value = jnp.dot(pick, tok_ref[...], preferred_element_type=F32).astype(BF16)
            for h in range(2):
                for w in range(4):
                    lo = h * half + (w % 2) * lane_half
                    xg[h, 0, w] = value[(w // 2) * row_half : (w // 2 + 1) * row_half, lo : lo + lane_half]
        else:
            value = jnp.dot(pick, own_half, preferred_element_type=F32).astype(BF16)
            for w in range(4):
                lo = (w % 2) * lane_half
                pk[k, w] = value[(w // 2) * row_half : (w // 2 + 1) * row_half, lo : lo + lane_half]

    pl.semaphore_wait(barrier, len(peers))

    quarter = z % 4
    a_copies, h_copies, b_copies = {}, {}, {}
    for k in FAR:
        a_copies[k] = remote(
            pk.at[k, quarter], xg.at[c, k, quarter], a_s.at[k, 0], a_r.at[k, 0], dev_y(-OFFSETS[k])
        )
        a_copies[k].start()
    for k in NEAR:
        a_copies[k] = remote(pk.at[k], xg.at[c, k], a_s.at[k, 0], a_r.at[k, 0], dev_y(-OFFSETS[k]))
        a_copies[k].start()

    for k in range(SLOTS):
        hit = code[k : k + 1, :] == row_id
        placed = jnp.where(hit, weight[k : k + 1, :], 0.0)
        high = placed.astype(BF16)
        pwh[pl.ds(k * rows, rows), :] = high
        pwl[pl.ds(k * rows, rows), :] = (placed - high.astype(F32)).astype(BF16)

    start = p * feats
    base = pl.multiple_of(jnp.minimum(start // 128 * 128, width - 256), 128)
    window = tok_ref[:, pl.ds(base, 256)].astype(F32)
    own_ref[...] = pltpu.roll(window, lax.rem(256 - (start - base), 256), 1)[:, :128]

    c_copies, d_copies, e_copies, f_copies, g_copies = {}, {}, {}, {}, {}

    def share_far(k):
        a_copies[k].wait_recv()
        block = xg.at[c, k, quarter]
        two_away = 2 * lax.rem(z + 2 + 4 * c, n_z) + c
        for i, dev in ((1, dev_z(1)), (2, dev_z(7)), (3, (two_away, y, x))):
            copy = remote(block, block, a_s.at[k, i], a_r.at[k, i], dev)
            copy.start()
            h_copies[k, i] = copy

    def to_partner(k):
        if k in FAR:
            for i in (1, 2, 3):
                h_copies[k, i].wait_recv()
        else:
            a_copies[k].wait_recv()
        b_copies[k] = remote(xg.at[c, k], xg.at[c, k], b_s.at[k], b_r.at[k], (partner, y, x))
        b_copies[k].start()

    totals = {}

    def prepare(k, h, own):
        g, q = k // PER, k % PER
        for rh in range(2):
            total = totals.get((k, rh), jnp.zeros((row_half, 1), F32))
            for lh in range(2):
                block = xg[h, k, 2 * rh + lh].astype(F32)
                total = total + jnp.sum(block * block, axis=-1, keepdims=True)
                if isinstance(h, int):
                    factor, lo = gains[2 * h + lh], h * half + lh * lane_half
                else:
                    factor = jnp.where(h == 0, gains[lh], gains[2 + lh])
                    lo = pl.multiple_of(h * half + lh * lane_half, 128)
                xn[g, pl.ds(q * rows + rh * row_half, row_half), pl.ds(lo, lane_half)] = (
                    block * factor
                ).astype(BF16)
            totals[k, rh] = total

    def prepare_other(k):
        b_copies[k].wait_recv()
        prepare(k, 1 - c, False)

    def stage_a(g):
        if g == 0:
            weight_copies[0].wait()
        gate = jnp.dot(xn[g], wu[...], preferred_element_type=F32)
        lanes = lax.broadcasted_iota(jnp.int32, (PER * rows, 128), 1)
        square = jnp.concatenate(
            [
                jnp.broadcast_to(totals[k, rh], (row_half, 128))
                for k in range(g * PER, (g + 1) * PER) for rh in range(2)
            ],
            axis=0,
        )
        high = square.astype(BF16).astype(F32)
        square = jnp.where(lanes < 64, high, square - high).astype(BF16)
        gate = gate.astype(BF16)
        for q in range(4):
            rs[g, q, :, pl.ds(0, units)] = gate[q * piece_rows : (q + 1) * piece_rows]
            rs[g, q, :, pl.ds(units, 128)] = square[q * piece_rows : (q + 1) * piece_rows]
        for j in range(1, 4):
            copy = remote(rs.at[g, lax.rem(x + j, n_x)], rr.at[g, j], c_s.at[g, j], c_r.at[g, j], dev_x(j))
            copy.start()
            c_copies[g, j] = copy

    def stage_b(g):
        total = rs[g, x].astype(F32)
        for j in range(1, 4):
            c_copies[g, j].wait_recv()
            total = total + rr[g, j].astype(F32)
        square = total[:, units : units + 1] + total[:, units + 64 : units + 65]
        scale = lax.rsqrt(square / (width * n_x) + 1e-05)
        gate = total[:, :units] * scale
        hb[g, x] = (gate / (1.0 + jnp.exp(-gate))).astype(BF16)
        for j in range(1, 4):
            copy = remote(hb.at[g, x], hb.at[g, x], d_s.at[g, j], d_r.at[g, j], dev_x(j))
            copy.start()
            d_copies[g, j] = copy

    def stage_c(g):
        for j in range(1, 4):
            d_copies[g, j].wait_recv()
        hidden = hb[g].reshape(4 * piece_rows, units)
        if g == 0:
            for copy in weight_copies[1:]:
                copy.wait()
        lanes = lax.broadcasted_iota(jnp.int32, (piece_rows, lane_group), 1)
        for part in range(wd.shape[0]):
            outs = jnp.dot(hidden, wd[part], preferred_element_type=F32)
            for r in range(4):
                packed = None
                for q in range(4):
                    piece = outs[q * piece_rows : (q + 1) * piece_rows]
                    shift = ((q - r) % 4) * feats
                    moved = piece if shift == 0 else pltpu.roll(piece, shift, 1)
                    packed = moved if packed is None else jnp.where(lanes >= q * feats, moved, packed)
                cs[g, r % 2, 2 * part + r // 2] = packed.astype(BF16)
            copy = remote(
                cs.at[g, 1 - c, pl.ds(2 * part, 2)], cr.at[g, pl.ds(2 * part, 2)],
                e_s.at[g, part], e_r.at[g, part], (partner, y, x),
            )
            copy.start()
            e_copies[g, part] = copy

    way = 1 - 2 * c

    def chip(n):
        return lax.rem(z + way * n + n_z, n_z)

    def partial_sum(g, n):
        to = chip(n)
        return cs[g, c, to].astype(F32) + cr[g, to].astype(F32)

    def send_z(g, slot, value, n):
        zs[g, slot] = value.astype(BF16)
        dev = (2 * chip(n) + c, y, x)
        copy = remote(zs.at[g, slot], zr.at[g, slot], f_s.at[g, slot], f_r.at[g, slot], dev)
        copy.start()
        f_copies[g, slot] = copy

    def arrived(g, slot):
        f_copies[g, slot].wait_recv()
        return zr[g, slot].astype(F32)

    def stage_d(g):
        for part in range(wd.shape[0]):
            e_copies[g, part].wait_recv()
        if g in RELAYED:
            for slot, to, via in ((5, 4, 2), (3, 3, 1), (4, -3, -1), (1, 1, 1), (2, -1, -1)):
                send_z(g, slot, partial_sum(g, to), via)
        else:
            for j in (4, 3, 5, 2, 6, 1, 7):
                send_z(g, j, partial_sum(g, j), j)

    def relay(g):
        if g in RELAYED:
            send_z(g, 7, partial_sum(g, -2) + arrived(g, 4), -2)
            send_z(g, 6, partial_sum(g, 2) + arrived(g, 3) + arrived(g, 5), 2)

    def stage_e(g):
        total = partial_sum(g, 0)
        for slot in (1, 2, 7, 6) if g in RELAYED else (1, 7, 2, 6, 3, 5, 4):
            total = total + arrived(g, slot)
        for k in range(g * PER, (g + 1) * PER):
            for i in range(4 // PER):
                q = (k % PER) * (4 // PER) + i
                moved = total if q == 0 else pltpu.roll(total, lane_group - q * feats, 1)
                block = moved[:, :128].astype(BF16)
                if k == 0:
                    ret[k, pl.ds(i * piece_rows, piece_rows)] = block
                else:
                    ys[k, pl.ds(i * piece_rows, piece_rows)] = block
            if k > 0:
                copy = remote(ys.at[k], ret.at[k], g_s.at[k], g_r.at[k], dev_y(OFFSETS[k]))
                copy.start()
                g_copies[k] = copy

    prepare(0, 0, True)
    prepare(0, 1, True)
    share_far(7)
    share_far(5)
    share_far(6)
    share_far(3)
    share_far(4)
    to_partner(1)
    prepare(1, c, True)
    to_partner(2)
    prepare(2, c, True)
    prepare_other(1)
    stage_a(0)
    to_partner(7)
    prepare(7, c, True)
    to_partner(6)
    prepare(6, c, True)
    prepare_other(7)
    prepare_other(6)
    stage_a(3)
    to_partner(5)
    prepare(5, c, True)
    to_partner(4)
    prepare(4, c, True)
    prepare_other(5)
    prepare_other(4)
    stage_a(2)
    stage_b(0)
    to_partner(3)
    prepare(3, c, True)
    prepare_other(3)
    prepare_other(2)
    stage_a(1)
    stage_b(3)
    stage_b(2)
    stage_c(0)
    stage_b(1)
    stage_d(0)
    stage_c(3)
    stage_d(3)
    stage_c(2)
    relay(0)
    stage_d(2)
    stage_c(1)
    relay(3)
    stage_d(1)
    stage_e(0)
    relay(2)
    stage_e(3)
    stage_e(2)
    stage_e(1)
    for k in range(1, SLOTS):
        g_copies[k].wait_recv()
    back = ret[...].reshape(SLOTS * rows, 128)
    dims = (((0,), (0,)), ((), ()))
    moe = lax.dot_general(pwh[...], back, dims, preferred_element_type=F32)
    moe = moe + lax.dot_general(pwl[...], back, dims, preferred_element_type=F32)
    out_ref[...] = (own_ref[:, :feats] + moe[:, :feats]).astype(BF16)
    for group in (a_copies, h_copies, b_copies, c_copies, d_copies, e_copies, f_copies, g_copies):
        for copy in group.values():
            copy.wait_send()


def on_device(tokens, norm_gain, up_w, down_w, expert_ids, gate_gap):
    micro, _, row_count, width = tokens.shape
    n_tok = micro * row_count
    rows = micro * CAP
    units = up_w.shape[2]
    pipe = lax.axis_size("pipe")
    n_z = pipe // 2
    feats = width // pipe
    lane_group = 4 * feats
    piece_rows = PER * rows // 4
    parts = width // lane_group
    flat = tokens.reshape(n_tok, width)
    ids = expert_ids.transpose(0, 1, 3, 2)
    vmem = pl.BlockSpec(memory_space=pltpu.VMEM)
    hbm = pl.BlockSpec(memory_space=pl.ANY)
    dma = pltpu.SemaphoreType.DMA
    result = pl.pallas_call(
        layer_kernel,
        out_shape=jax.ShapeDtypeStruct((n_tok, feats), BF16),
        in_specs=[hbm] * 6,
        out_specs=vmem,
        scratch_shapes=[
            pltpu.VMEM((n_tok, width), BF16),
            pltpu.VMEM((n_tok, 128), F32),
            pltpu.VMEM((width // 128, 128), F32),
            pltpu.VMEM(ids.shape, jnp.int32),
            pltpu.VMEM(gate_gap.shape, F32),
            pltpu.VMEM((width, units), BF16),
            pltpu.VMEM((parts, units, lane_group), BF16),
            pltpu.VMEM((SLOTS, 4, rows // 2, width // 4), BF16),
            pltpu.VMEM((2, SLOTS, 4, rows // 2, width // 4), BF16),
            pltpu.VMEM((GROUPS, PER * rows, width), BF16),
            pltpu.VMEM((GROUPS, 4, piece_rows, units + 128), BF16),
            pltpu.VMEM((GROUPS, 4, piece_rows, units + 128), BF16),
            pltpu.VMEM((GROUPS, 4, piece_rows, units), BF16),
            pltpu.VMEM((GROUPS, 2, n_z, piece_rows, lane_group), BF16),
            pltpu.VMEM((GROUPS, n_z, piece_rows, lane_group), BF16),
            pltpu.VMEM((GROUPS, n_z, piece_rows, lane_group), BF16),
            pltpu.VMEM((GROUPS, n_z, piece_rows, lane_group), BF16),
            pltpu.VMEM((SLOTS, rows, 128), BF16),
            pltpu.VMEM((SLOTS, rows, 128), BF16),
            pltpu.VMEM((SLOTS * rows, n_tok), BF16),
            pltpu.VMEM((SLOTS * rows, n_tok), BF16),
            dma((5 + parts,)),
            dma((SLOTS, 4)), dma((SLOTS, 4)),
            dma((SLOTS,)), dma((SLOTS,)),
            dma((GROUPS, 4)), dma((GROUPS, 4)),
            dma((GROUPS, 4)), dma((GROUPS, 4)),
            dma((GROUPS, parts)), dma((GROUPS, parts)),
            dma((GROUPS, n_z)), dma((GROUPS, n_z)),
            dma((SLOTS,)), dma((SLOTS,)),
        ],
        compiler_params=pltpu.CompilerParams(
            collective_id=0, has_side_effects=True, vmem_limit_bytes=56 * 1024 * 1024
        ),
        name="expert_layer",
    )(flat, norm_gain.reshape(width // 128, 128), ids, gate_gap, up_w[0], down_w[0])
    return result.reshape(micro, 1, row_count, feats)


def solution(mesh):
    return jax.shard_map(
        on_device,
        mesh=mesh,
        in_specs=(
            P(None, "expert", None, "dp"),
            P("dp"),
            P("expert", "dp", "pipe"),
            P("expert", "pipe", "dp"),
            P(None, "expert", None, None),
            P(None, "expert", None),
        ),
        out_specs=P(None, "expert", None, ("dp", "pipe")),
        check_vma=False,
    )
```

```python
import jax
import jax.numpy as jnp
from jax import lax
from jax.experimental import pallas as pl
from jax.experimental.pallas import tpu as pltpu
from jax.sharding import PartitionSpec as P

MESH = pl.DeviceIdType.MESH
OFFSETS = (0, 1, -1, 2, -2, 3, -3, 4)
SLOTS = 8
PER = 2
GROUPS = SLOTS // PER
NEAR = (1, 2, 3, 4)
FAR = (7, 5, 6)
RELAYED = (0, 3, 2)
CAP = 6
F32 = jnp.float32
BF16 = jnp.bfloat16


def layer_kernel(
    tok_hbm, gain_hbm, ids_hbm, gap_hbm, up_hbm, down_hbm, out_ref,
    tok_ref, own_ref, gain_ref, ids_ref, gap_ref, wu, wd, pk, xg, xn, rs, rr, hb, cs, cr, zs, zr, ys, ret, pwh, pwl,
    w_sem, a_s, a_r, b_s, b_r, c_s, c_r, d_s, d_r, e_s, e_r, f_s, f_r, g_s, g_r,
):
    p = lax.axis_index("pipe")
    y = lax.axis_index("expert")
    x = lax.axis_index("dp")
    n_y = lax.axis_size("expert")
    n_x = lax.axis_size("dp")
    n_z = lax.axis_size("pipe") // 2
    z = p // 2
    c = p % 2
    partner = 2 * z + 1 - c
    n_tok, width = tok_ref.shape
    half = width // 2
    rows = n_tok // 16 * CAP
    row_half, lane_half = pk.shape[2:]
    units = wu.shape[1]
    feats = width // (2 * n_z)
    lane_group = 4 * feats
    piece_rows = PER * rows // 4

    def dev_y(offset):
        return (p, lax.rem(y + offset + n_y, n_y), x)

    def dev_x(j):
        return (p, y, lax.rem(x + j, n_x))

    def dev_z(j):
        return (2 * lax.rem(z + j, n_z) + c, y, x)

    def remote(src, dst, s, r, dev):
        return pltpu.make_async_remote_copy(
            src_ref=src, dst_ref=dst, send_sem=s, recv_sem=r, device_id=dev, device_id_type=MESH
        )

    barrier = pltpu.get_barrier_semaphore()
    peers = [dev_y(o) for o in OFFSETS[1:]] + [dev_x(j) for j in range(1, 4)]
    peers += [dev_z(j) for j in range(1, 8)] + [(partner, y, x)]
    for dev in peers:
        pl.semaphore_signal(barrier, inc=1, device_id=dev, device_id_type=MESH)

    small_copies = [
        pltpu.make_async_copy(src, dst, w_sem.at[i])
        for i, (src, dst) in enumerate(((ids_hbm, ids_ref), (gap_hbm, gap_ref), (gain_hbm, gain_ref)))
    ]
    token_copy = pltpu.make_async_copy(tok_hbm, tok_ref, w_sem.at[3])
    for copy in small_copies:
        copy.start()
    token_copy.start()
    weight_copies = [pltpu.make_async_copy(up_hbm, wu, w_sem.at[4])]
    for part in range(wd.shape[0]):
        weight_copies.append(
            pltpu.make_async_copy(
                down_hbm.at[:, pl.ds(part * lane_group, lane_group)], wd.at[part], w_sem.at[5 + part]
            )
        )
    for copy in weight_copies:
        copy.start()

    sub = lax.broadcasted_iota(jnp.int32, (SLOTS, n_tok), 0)
    lane = lax.broadcasted_iota(jnp.int32, (SLOTS, n_tok), 1)
    offset = jnp.zeros_like(sub)
    for k in range(SLOTS):
        offset = jnp.where(sub == k, OFFSETS[k], offset)
    expert_of = y - offset
    expert_of = jnp.where(expert_of < 0, expert_of + n_y, expert_of)
    expert_of = jnp.where(expert_of >= n_y, expert_of - n_y, expert_of).astype(F32)
    spread = lax.broadcasted_iota(jnp.int32, (16, n_tok), 1) % 16
    spread = jnp.where(spread == lax.broadcasted_iota(jnp.int32, (16, n_tok), 0), 1.0, 0.0)

    def as_row(blocks):
        wide = jnp.dot(
            jnp.concatenate(blocks, axis=0), spread,
            preferred_element_type=F32, precision=lax.Precision.HIGHEST,
        )
        return jnp.sum(jnp.where(lane // 16 == sub, wide, 0.0), axis=0, keepdims=True)

    micros = range(n_tok // 16)
    for copy in small_copies:
        copy.wait()
    first = as_row([ids_ref[m, 0, 0:1, :].astype(F32) for m in micros]) == expert_of
    second = as_row([ids_ref[m, 0, 1:2, :].astype(F32) for m in micros]) == expert_of
    share = 1.0 / (1.0 + jnp.exp(-as_row([gap_ref[m] for m in micros])))
    weight = jnp.where(first, share, 0.0) + jnp.where(second, 1.0 - share, 0.0)
    member = first | second
    before = lax.broadcasted_iota(jnp.int32, (n_tok, n_tok), 0)
    token = lax.broadcasted_iota(jnp.int32, (n_tok, n_tok), 1)
    block_of = (token // 16) == (before // 16)
    earlier = jnp.where(block_of & (before < token), 1.0, 0.0).astype(BF16)
    rank = jnp.dot(jnp.where(member, 1.0, 0.0).astype(BF16), earlier, preferred_element_type=F32)
    code = jnp.where(member, rank + ((lane // 16) * CAP).astype(F32), -1.0)
    row_id = lax.broadcasted_iota(jnp.int32, (rows, n_tok), 0).astype(F32)
    lo_half = pl.multiple_of(c * half, 128)
    token_copy.wait()
    own_half = tok_ref[:, pl.ds(lo_half, half)]
    gain = jnp.concatenate([gain_ref[i : i + 1, :] for i in range(width // 128)], axis=1)
    gains = [gain[:, i * lane_half : (i + 1) * lane_half] for i in range(width // lane_half)]
    for k in range(SLOTS):
        hit = code[k : k + 1, :] == row_id
        pick = jnp.where(hit, 1.0, 0.0).astype(BF16)
        if k == 0:
            value = jnp.dot(pick, tok_ref[...], preferred_element_type=F32).astype(BF16)
            for h in range(2):
                for w in range(4):
                    lo = h * half + (w % 2) * lane_half
                    xg[h, 0, w] = value[(w // 2) * row_half : (w // 2 + 1) * row_half, lo : lo + lane_half]
        else:
            value = jnp.dot(pick, own_half, preferred_element_type=F32).astype(BF16)
            for w in range(4):
                lo = (w % 2) * lane_half
                pk[k, w] = value[(w // 2) * row_half : (w // 2 + 1) * row_half, lo : lo + lane_half]

    pl.semaphore_wait(barrier, len(peers))

    quarter = z % 4
    a_copies, h_copies, b_copies = {}, {}, {}
    for k in FAR:
        a_copies[k] = remote(
            pk.at[k, quarter], xg.at[c, k, quarter], a_s.at[k, 0], a_r.at[k, 0], dev_y(-OFFSETS[k])
        )
        a_copies[k].start()
    for k in NEAR:
        a_copies[k] = remote(pk.at[k], xg.at[c, k], a_s.at[k, 0], a_r.at[k, 0], dev_y(-OFFSETS[k]))
        a_copies[k].start()

    place = []
    for k in range(SLOTS):
        hit = code[k : k + 1, :] == row_id
        placed = jnp.where(hit, weight[k : k + 1, :], 0.0)
        place.append(placed)
    placed = jnp.concatenate(place, axis=0).T
    high = placed.astype(BF16)
    pwh[...] = high
    pwl[...] = (placed - high.astype(F32)).astype(BF16)

    start = p * feats
    base = pl.multiple_of(jnp.minimum(start // 128 * 128, width - 256), 128)
    window = tok_ref[:, pl.ds(base, 256)].astype(F32)
    own_ref[...] = pltpu.roll(window, lax.rem(256 - (start - base), 256), 1)[:, :128]

    c_copies, d_copies, e_copies, f_copies, g_copies = {}, {}, {}, {}, {}

    def share_far(k):
        a_copies[k].wait_recv()
        block = xg.at[c, k, quarter]
        two_away = 2 * lax.rem(z + 2 + 4 * c, n_z) + c
        for i, dev in ((1, dev_z(1)), (2, dev_z(7)), (3, (two_away, y, x))):
            copy = remote(block, block, a_s.at[k, i], a_r.at[k, i], dev)
            copy.start()
            h_copies[k, i] = copy

    def to_partner(k):
        if k in FAR:
            for i in (1, 2, 3):
                h_copies[k, i].wait_recv()
        else:
            a_copies[k].wait_recv()
        b_copies[k] = remote(xg.at[c, k], xg.at[c, k], b_s.at[k], b_r.at[k], (partner, y, x))
        b_copies[k].start()

    totals = {}

    def prepare(k, h, own):
        g, q = k // PER, k % PER
        for rh in range(2):
            total = totals.get((k, rh), jnp.zeros((row_half, 1), F32))
            for lh in range(2):
                block = xg[h, k, 2 * rh + lh].astype(F32)
                total = total + jnp.sum(block * block, axis=-1, keepdims=True)
                if isinstance(h, int):
                    factor, lo = gains[2 * h + lh], h * half + lh * lane_half
                else:
                    factor = jnp.where(h == 0, gains[lh], gains[2 + lh])
                    lo = pl.multiple_of(h * half + lh * lane_half, 128)
                xn[g, pl.ds(q * rows + rh * row_half, row_half), pl.ds(lo, lane_half)] = (
                    block * factor
                ).astype(BF16)
            totals[k, rh] = total

    def prepare_other(k):
        b_copies[k].wait_recv()
        prepare(k, 1 - c, False)

    def stage_a(g):
        if g == 0:
            weight_copies[0].wait()
        gate = jnp.dot(xn[g], wu[...], preferred_element_type=F32)
        lanes = lax.broadcasted_iota(jnp.int32, (PER * rows, 128), 1)
        square = jnp.concatenate(
            [
                jnp.broadcast_to(totals[k, rh], (row_half, 128))
                for k in range(g * PER, (g + 1) * PER) for rh in range(2)
            ],
            axis=0,
        )
        high = square.astype(BF16).astype(F32)
        square = jnp.where(lanes < 64, high, square - high).astype(BF16)
        gate = gate.astype(BF16)
        for q in range(4):
            rs[g, q, :, pl.ds(0, units)] = gate[q * piece_rows : (q + 1) * piece_rows]
            rs[g, q, :, pl.ds(units, 128)] = square[q * piece_rows : (q + 1) * piece_rows]
        for j in range(1, 4):
            copy = remote(rs.at[g, lax.rem(x + j, n_x)], rr.at[g, j], c_s.at[g, j], c_r.at[g, j], dev_x(j))
            copy.start()
            c_copies[g, j] = copy

    def stage_b(g):
        total = rs[g, x].astype(F32)
        for j in range(1, 4):
            c_copies[g, j].wait_recv()
            total = total + rr[g, j].astype(F32)
        square = total[:, units : units + 1] + total[:, units + 64 : units + 65]
        scale = lax.rsqrt(square / (width * n_x) + 1e-05)
        gate = total[:, :units] * scale
        hb[g, x] = (gate / (1.0 + jnp.exp(-gate))).astype(BF16)
        for j in range(1, 4):
            copy = remote(hb.at[g, x], hb.at[g, x], d_s.at[g, j], d_r.at[g, j], dev_x(j))
            copy.start()
            d_copies[g, j] = copy

    def stage_c(g):
        for j in range(1, 4):
            d_copies[g, j].wait_recv()
        hidden = hb[g].reshape(4 * piece_rows, units)
        if g == 0:
            for copy in weight_copies[1:]:
                copy.wait()
        lanes = lax.broadcasted_iota(jnp.int32, (piece_rows, lane_group), 1)
        for part in range(wd.shape[0]):
            outs = jnp.dot(hidden, wd[part], preferred_element_type=F32)
            for r in range(4):
                packed = None
                for q in range(4):
                    piece = outs[q * piece_rows : (q + 1) * piece_rows]
                    shift = ((q - r) % 4) * feats
                    moved = piece if shift == 0 else pltpu.roll(piece, shift, 1)
                    packed = moved if packed is None else jnp.where(lanes >= q * feats, moved, packed)
                cs[g, r % 2, 2 * part + r // 2] = packed.astype(BF16)
            copy = remote(
                cs.at[g, 1 - c, pl.ds(2 * part, 2)], cr.at[g, pl.ds(2 * part, 2)],
                e_s.at[g, part], e_r.at[g, part], (partner, y, x),
            )
            copy.start()
            e_copies[g, part] = copy

    way = 1 - 2 * c

    def chip(n):
        return lax.rem(z + way * n + n_z, n_z)

    def partial_sum(g, n):
        to = chip(n)
        return cs[g, c, to].astype(F32) + cr[g, to].astype(F32)

    def send_z(g, slot, value, n):
        zs[g, slot] = value.astype(BF16)
        dev = (2 * chip(n) + c, y, x)
        copy = remote(zs.at[g, slot], zr.at[g, slot], f_s.at[g, slot], f_r.at[g, slot], dev)
        copy.start()
        f_copies[g, slot] = copy

    def arrived(g, slot):
        f_copies[g, slot].wait_recv()
        return zr[g, slot].astype(F32)

    def stage_d(g):
        for part in range(wd.shape[0]):
            e_copies[g, part].wait_recv()
        if g in RELAYED:
            for slot, to, via in ((5, 4, 2), (3, 3, 1), (4, -3, -1), (1, 1, 1), (2, -1, -1)):
                send_z(g, slot, partial_sum(g, to), via)
        else:
            for j in (4, 3, 5, 2, 6, 1, 7):
                send_z(g, j, partial_sum(g, j), j)

    def relay(g):
        if g in RELAYED:
            send_z(g, 7, partial_sum(g, -2) + arrived(g, 4), -2)
            send_z(g, 6, partial_sum(g, 2) + arrived(g, 3) + arrived(g, 5), 2)

    def stage_e(g):
        total = partial_sum(g, 0)
        for slot in (1, 2, 7, 6) if g in RELAYED else (1, 7, 2, 6, 3, 5, 4):
            total = total + arrived(g, slot)
        for k in range(g * PER, (g + 1) * PER):
            for i in range(4 // PER):
                q = (k % PER) * (4 // PER) + i
                moved = total if q == 0 else pltpu.roll(total, lane_group - q * feats, 1)
                block = moved[:, :128].astype(BF16)
                if k == 0:
                    ret[k, pl.ds(i * piece_rows, piece_rows)] = block
                else:
                    ys[k, pl.ds(i * piece_rows, piece_rows)] = block
            if k > 0:
                copy = remote(ys.at[k], ret.at[k], g_s.at[k], g_r.at[k], dev_y(OFFSETS[k]))
                copy.start()
                g_copies[k] = copy

    prepare(0, 0, True)
    prepare(0, 1, True)
    share_far(7)
    share_far(5)
    share_far(6)
    to_partner(1)
    prepare(1, c, True)
    to_partner(2)
    prepare(2, c, True)
    prepare_other(1)
    stage_a(0)
    to_partner(7)
    prepare(7, c, True)
    to_partner(6)
    prepare(6, c, True)
    prepare_other(7)
    prepare_other(6)
    stage_a(3)
    to_partner(5)
    prepare(5, c, True)
    to_partner(4)
    prepare(4, c, True)
    prepare_other(5)
    prepare_other(4)
    stage_a(2)
    stage_b(0)
    to_partner(3)
    prepare(3, c, True)
    prepare_other(3)
    prepare_other(2)
    stage_a(1)
    stage_b(3)
    stage_b(2)
    stage_c(0)
    stage_b(1)
    stage_c(3)
    stage_d(0)
    stage_c(2)
    stage_d(3)
    stage_c(1)
    stage_d(2)
    relay(0)
    stage_d(1)
    relay(3)
    relay(2)
    stage_e(0)
    stage_e(3)
    stage_e(2)
    stage_e(1)
    for k in range(1, SLOTS):
        g_copies[k].wait_recv()
    back = ret[...].reshape(SLOTS * rows, 128)
    moe = jnp.dot(pwh[...], back, preferred_element_type=F32)
    moe = moe + jnp.dot(pwl[...], back, preferred_element_type=F32)
    out_ref[...] = (own_ref[:, :feats] + moe[:, :feats]).astype(BF16)
    for group in (a_copies, h_copies, b_copies, c_copies, d_copies, e_copies, f_copies, g_copies):
        for copy in group.values():
            copy.wait_send()


def on_device(tokens, norm_gain, up_w, down_w, expert_ids, gate_gap):
    micro, _, row_count, width = tokens.shape
    n_tok = micro * row_count
    rows = micro * CAP
    units = up_w.shape[2]
    pipe = lax.axis_size("pipe")
    n_z = pipe // 2
    feats = width // pipe
    lane_group = 4 * feats
    piece_rows = PER * rows // 4
    parts = width // lane_group
    flat = tokens.reshape(n_tok, width)
    ids = expert_ids.transpose(0, 1, 3, 2)
    vmem = pl.BlockSpec(memory_space=pltpu.VMEM)
    hbm = pl.BlockSpec(memory_space=pl.ANY)
    dma = pltpu.SemaphoreType.DMA
    result = pl.pallas_call(
        layer_kernel,
        out_shape=jax.ShapeDtypeStruct((n_tok, feats), BF16),
        in_specs=[hbm] * 6,
        out_specs=vmem,
        scratch_shapes=[
            pltpu.VMEM((n_tok, width), BF16),
            pltpu.VMEM((n_tok, 128), F32),
            pltpu.VMEM((width // 128, 128), F32),
            pltpu.VMEM(ids.shape, jnp.int32),
            pltpu.VMEM(gate_gap.shape, F32),
            pltpu.VMEM((width, units), BF16),
            pltpu.VMEM((parts, units, lane_group), BF16),
            pltpu.VMEM((SLOTS, 4, rows // 2, width // 4), BF16),
            pltpu.VMEM((2, SLOTS, 4, rows // 2, width // 4), BF16),
            pltpu.VMEM((GROUPS, PER * rows, width), BF16),
            pltpu.VMEM((GROUPS, 4, piece_rows, units + 128), BF16),
            pltpu.VMEM((GROUPS, 4, piece_rows, units + 128), BF16),
            pltpu.VMEM((GROUPS, 4, piece_rows, units), BF16),
            pltpu.VMEM((GROUPS, 2, n_z, piece_rows, lane_group), BF16),
            pltpu.VMEM((GROUPS, n_z, piece_rows, lane_group), BF16),
            pltpu.VMEM((GROUPS, n_z, piece_rows, lane_group), BF16),
            pltpu.VMEM((GROUPS, n_z, piece_rows, lane_group), BF16),
            pltpu.VMEM((SLOTS, rows, 128), BF16),
            pltpu.VMEM((SLOTS, rows, 128), BF16),
            pltpu.VMEM((n_tok, SLOTS * rows), BF16),
            pltpu.VMEM((n_tok, SLOTS * rows), BF16),
            dma((5 + parts,)),
            dma((SLOTS, 4)), dma((SLOTS, 4)),
            dma((SLOTS,)), dma((SLOTS,)),
            dma((GROUPS, 4)), dma((GROUPS, 4)),
            dma((GROUPS, 4)), dma((GROUPS, 4)),
            dma((GROUPS, parts)), dma((GROUPS, parts)),
            dma((GROUPS, n_z)), dma((GROUPS, n_z)),
            dma((SLOTS,)), dma((SLOTS,)),
        ],
        compiler_params=pltpu.CompilerParams(
            collective_id=0, has_side_effects=True, vmem_limit_bytes=56 * 1024 * 1024
        ),
        name="expert_layer",
    )(flat, norm_gain.reshape(width // 128, 128), ids, gate_gap, up_w[0], down_w[0])
    return result.reshape(micro, 1, row_count, feats)


def solution(mesh):
    return jax.shard_map(
        on_device,
        mesh=mesh,
        in_specs=(
            P(None, "expert", None, "dp"),
            P("dp"),
            P("expert", "dp", "pipe"),
            P("expert", "pipe", "dp"),
            P(None, "expert", None, None),
            P(None, "expert", None),
        ),
        out_specs=P(None, "expert", None, ("dp", "pipe")),
        check_vma=False,
    )
```

```python
import jax
import jax.numpy as jnp
from jax import lax
from jax.experimental import pallas as pl
from jax.experimental.pallas import tpu as pltpu
from jax.sharding import PartitionSpec as P

MESH = pl.DeviceIdType.MESH
OFFSETS = (0, 1, -1, 2, -2, 3, -3, 4)
SLOTS = 8
PER = 2
GROUPS = SLOTS // PER
NEAR = (1, 2, 3, 4)
FAR = (7, 5, 6)
RELAYED = (0, 3, 2)
CAP = 6
F32 = jnp.float32
BF16 = jnp.bfloat16


def layer_kernel(
    tok_hbm, gain_hbm, ids_hbm, gap_hbm, up_hbm, down_hbm, out_ref,
    tok_ref, own_ref, gain_ref, ids_ref, gap_ref, wu, wd, pk, xg, xn, rs, rr, hb, cs, cr, zs, zr, ys, ret, pwh, pwl,
    w_sem, a_s, a_r, b_s, b_r, c_s, c_r, d_s, d_r, e_s, e_r, f_s, f_r, g_s, g_r,
):
    p = lax.axis_index("pipe")
    y = lax.axis_index("expert")
    x = lax.axis_index("dp")
    n_y = lax.axis_size("expert")
    n_x = lax.axis_size("dp")
    n_z = lax.axis_size("pipe") // 2
    z = p // 2
    c = p % 2
    partner = 2 * z + 1 - c
    n_tok, width = tok_ref.shape
    half = width // 2
    rows = n_tok // 16 * CAP
    row_half, lane_half = pk.shape[2:]
    units = wu.shape[1]
    feats = width // (2 * n_z)
    lane_group = 4 * feats
    piece_rows = PER * rows // 4

    def dev_y(offset):
        return (p, lax.rem(y + offset + n_y, n_y), x)

    def dev_x(j):
        return (p, y, lax.rem(x + j, n_x))

    def dev_z(j):
        return (2 * lax.rem(z + j, n_z) + c, y, x)

    def remote(src, dst, s, r, dev):
        return pltpu.make_async_remote_copy(
            src_ref=src, dst_ref=dst, send_sem=s, recv_sem=r, device_id=dev, device_id_type=MESH
        )

    barrier = pltpu.get_barrier_semaphore()
    peers = []
    for o, j in zip(OFFSETS[:0:-1], (4, 3, 5, 2, 6, 1, 7)):
        peers += [dev_y(o), dev_z(j)]
    peers += [dev_x(j) for j in (2, 1, 3)] + [(partner, y, x)]
    for dev in peers:
        pl.semaphore_signal(barrier, inc=1, device_id=dev, device_id_type=MESH)

    small_copies = [
        pltpu.make_async_copy(src, dst, w_sem.at[i])
        for i, (src, dst) in enumerate(((ids_hbm, ids_ref), (gap_hbm, gap_ref), (gain_hbm, gain_ref)))
    ]
    token_copy = pltpu.make_async_copy(tok_hbm, tok_ref, w_sem.at[3])
    for copy in small_copies:
        copy.start()
    token_copy.start()
    weight_copies = [pltpu.make_async_copy(up_hbm, wu, w_sem.at[4])]
    for part in range(wd.shape[0]):
        weight_copies.append(
            pltpu.make_async_copy(
                down_hbm.at[:, pl.ds(part * lane_group, lane_group)], wd.at[part], w_sem.at[5 + part]
            )
        )
    for copy in weight_copies:
        copy.start()

    sub = lax.broadcasted_iota(jnp.int32, (SLOTS, n_tok), 0)
    lane = lax.broadcasted_iota(jnp.int32, (SLOTS, n_tok), 1)
    offset = jnp.zeros_like(sub)
    for k in range(SLOTS):
        offset = jnp.where(sub == k, OFFSETS[k], offset)
    expert_of = y - offset
    expert_of = jnp.where(expert_of < 0, expert_of + n_y, expert_of)
    expert_of = jnp.where(expert_of >= n_y, expert_of - n_y, expert_of).astype(F32)
    spread = lax.broadcasted_iota(jnp.int32, (16, n_tok), 1) % 16
    spread = jnp.where(spread == lax.broadcasted_iota(jnp.int32, (16, n_tok), 0), 1.0, 0.0)

    def as_row(blocks):
        wide = jnp.dot(
            jnp.concatenate(blocks, axis=0), spread,
            preferred_element_type=F32, precision=lax.Precision.HIGHEST,
        )
        return jnp.sum(jnp.where(lane // 16 == sub, wide, 0.0), axis=0, keepdims=True)

    micros = range(n_tok // 16)
    for copy in small_copies:
        copy.wait()
    first = as_row([ids_ref[m, 0, 0:1, :].astype(F32) for m in micros]) == expert_of
    second = as_row([ids_ref[m, 0, 1:2, :].astype(F32) for m in micros]) == expert_of
    share = 1.0 / (1.0 + jnp.exp(-as_row([gap_ref[m] for m in micros])))
    weight = jnp.where(first, share, 0.0) + jnp.where(second, 1.0 - share, 0.0)
    member = first | second
    before = lax.broadcasted_iota(jnp.int32, (n_tok, n_tok), 0)
    token = lax.broadcasted_iota(jnp.int32, (n_tok, n_tok), 1)
    block_of = (token // 16) == (before // 16)
    earlier = jnp.where(block_of & (before < token), 1.0, 0.0).astype(BF16)
    rank = jnp.dot(jnp.where(member, 1.0, 0.0).astype(BF16), earlier, preferred_element_type=F32)
    code = jnp.where(member, rank + ((lane // 16) * CAP).astype(F32), -1.0)
    row_id = lax.broadcasted_iota(jnp.int32, (rows, n_tok), 0).astype(F32)
    lo_half = pl.multiple_of(c * half, 128)
    token_copy.wait()
    own_half = tok_ref[:, pl.ds(lo_half, half)]
    gain = jnp.concatenate([gain_ref[i : i + 1, :] for i in range(width // 128)], axis=1)
    gains = [gain[:, i * lane_half : (i + 1) * lane_half] for i in range(width // lane_half)]
    for k in range(SLOTS):
        hit = code[k : k + 1, :] == row_id
        pick = jnp.where(hit, 1.0, 0.0).astype(BF16)
        if k == 0:
            value = jnp.dot(pick, tok_ref[...], preferred_element_type=F32).astype(BF16)
            for h in range(2):
                for w in range(4):
                    lo = h * half + (w % 2) * lane_half
                    xg[h, 0, w] = value[(w // 2) * row_half : (w // 2 + 1) * row_half, lo : lo + lane_half]
        else:
            value = jnp.dot(pick, own_half, preferred_element_type=F32).astype(BF16)
            for w in range(4):
                lo = (w % 2) * lane_half
                pk[k, w] = value[(w // 2) * row_half : (w // 2 + 1) * row_half, lo : lo + lane_half]

    pl.semaphore_wait(barrier, len(peers))

    quarter = z % 4
    a_copies, h_copies, b_copies = {}, {}, {}
    for k in FAR:
        a_copies[k] = remote(
            pk.at[k, quarter], xg.at[c, k, quarter], a_s.at[k, 0], a_r.at[k, 0], dev_y(-OFFSETS[k])
        )
        a_copies[k].start()
    for k in NEAR:
        a_copies[k] = remote(pk.at[k], xg.at[c, k], a_s.at[k, 0], a_r.at[k, 0], dev_y(-OFFSETS[k]))
        a_copies[k].start()

    place = []
    for k in range(SLOTS):
        hit = code[k : k + 1, :] == row_id
        placed = jnp.where(hit, weight[k : k + 1, :], 0.0)
        place.append(placed)
    placed = jnp.concatenate(place, axis=0).T
    high = placed.astype(BF16)
    pwh[...] = high
    pwl[...] = (placed - high.astype(F32)).astype(BF16)

    start = p * feats
    base = pl.multiple_of(jnp.minimum(start // 128 * 128, width - 256), 128)
    window = tok_ref[:, pl.ds(base, 256)].astype(F32)
    own_ref[...] = pltpu.roll(window, lax.rem(256 - (start - base), 256), 1)[:, :128]

    c_copies, d_copies, e_copies, f_copies, g_copies = {}, {}, {}, {}, {}

    def share_far(k):
        a_copies[k].wait_recv()
        block = xg.at[c, k, quarter]
        two_away = 2 * lax.rem(z + 2 + 4 * c, n_z) + c
        for i, dev in ((1, dev_z(1)), (2, dev_z(7)), (3, (two_away, y, x))):
            copy = remote(block, block, a_s.at[k, i], a_r.at[k, i], dev)
            copy.start()
            h_copies[k, i] = copy

    def to_partner(k):
        if k in FAR:
            for i in (1, 2, 3):
                h_copies[k, i].wait_recv()
        else:
            a_copies[k].wait_recv()
        b_copies[k] = remote(xg.at[c, k], xg.at[c, k], b_s.at[k], b_r.at[k], (partner, y, x))
        b_copies[k].start()

    totals = {}

    def prepare(k, h, own):
        g, q = k // PER, k % PER
        for rh in range(2):
            total = totals.get((k, rh), jnp.zeros((row_half, 1), F32))
            for lh in range(2):
                block = xg[h, k, 2 * rh + lh].astype(F32)
                total = total + jnp.sum(block * block, axis=-1, keepdims=True)
                if isinstance(h, int):
                    factor, lo = gains[2 * h + lh], h * half + lh * lane_half
                else:
                    factor = jnp.where(h == 0, gains[lh], gains[2 + lh])
                    lo = pl.multiple_of(h * half + lh * lane_half, 128)
                xn[g, pl.ds(q * rows + rh * row_half, row_half), pl.ds(lo, lane_half)] = (
                    block * factor
                ).astype(BF16)
            totals[k, rh] = total

    def prepare_other(k):
        b_copies[k].wait_recv()
        prepare(k, 1 - c, False)

    def stage_a(g):
        if g == 0:
            weight_copies[0].wait()
        gate = jnp.dot(xn[g], wu[...], preferred_element_type=F32)
        lanes = lax.broadcasted_iota(jnp.int32, (PER * rows, 128), 1)
        square = jnp.concatenate(
            [
                jnp.broadcast_to(totals[k, rh], (row_half, 128))
                for k in range(g * PER, (g + 1) * PER) for rh in range(2)
            ],
            axis=0,
        )
        high = square.astype(BF16).astype(F32)
        square = jnp.where(lanes < 64, high, square - high).astype(BF16)
        gate = gate.astype(BF16)
        for q in range(4):
            rs[g, q, :, pl.ds(0, units)] = gate[q * piece_rows : (q + 1) * piece_rows]
            rs[g, q, :, pl.ds(units, 128)] = square[q * piece_rows : (q + 1) * piece_rows]
        for j in range(1, 4):
            copy = remote(rs.at[g, lax.rem(x + j, n_x)], rr.at[g, j], c_s.at[g, j], c_r.at[g, j], dev_x(j))
            copy.start()
            c_copies[g, j] = copy

    def stage_b(g):
        total = rs[g, x].astype(F32)
        for j in range(1, 4):
            c_copies[g, j].wait_recv()
            total = total + rr[g, j].astype(F32)
        square = total[:, units : units + 1] + total[:, units + 64 : units + 65]
        scale = lax.rsqrt(square / (width * n_x) + 1e-05)
        gate = total[:, :units] * scale
        hb[g, x] = (gate / (1.0 + jnp.exp(-gate))).astype(BF16)
        for j in range(1, 4):
            copy = remote(hb.at[g, x], hb.at[g, x], d_s.at[g, j], d_r.at[g, j], dev_x(j))
            copy.start()
            d_copies[g, j] = copy

    def stage_c(g):
        for j in range(1, 4):
            d_copies[g, j].wait_recv()
        hidden = hb[g].reshape(4 * piece_rows, units)
        if g == 0:
            for copy in weight_copies[1:]:
                copy.wait()
        lanes = lax.broadcasted_iota(jnp.int32, (piece_rows, lane_group), 1)
        for part in range(wd.shape[0]):
            outs = jnp.dot(hidden, wd[part], preferred_element_type=F32)
            for r in range(4):
                packed = None
                for q in range(4):
                    piece = outs[q * piece_rows : (q + 1) * piece_rows]
                    shift = ((q - r) % 4) * feats
                    moved = piece if shift == 0 else pltpu.roll(piece, shift, 1)
                    packed = moved if packed is None else jnp.where(lanes >= q * feats, moved, packed)
                cs[g, r % 2, 2 * part + r // 2] = packed.astype(BF16)
            copy = remote(
                cs.at[g, 1 - c, pl.ds(2 * part, 2)], cr.at[g, pl.ds(2 * part, 2)],
                e_s.at[g, part], e_r.at[g, part], (partner, y, x),
            )
            copy.start()
            e_copies[g, part] = copy

    way = 1 - 2 * c

    def chip(n):
        return lax.rem(z + way * n + n_z, n_z)

    def partial_sum(g, n):
        to = chip(n)
        return cs[g, c, to].astype(F32) + cr[g, to].astype(F32)

    def send_z(g, slot, value, n):
        zs[g, slot] = value.astype(BF16)
        dev = (2 * chip(n) + c, y, x)
        copy = remote(zs.at[g, slot], zr.at[g, slot], f_s.at[g, slot], f_r.at[g, slot], dev)
        copy.start()
        f_copies[g, slot] = copy

    def arrived(g, slot):
        f_copies[g, slot].wait_recv()
        return zr[g, slot].astype(F32)

    def stage_d(g):
        for part in range(wd.shape[0]):
            e_copies[g, part].wait_recv()
        if g in RELAYED:
            for slot, to, via in ((5, 4, 2), (4, -3, -1), (3, 3, 1), (1, 1, 1), (2, -1, -1)):
                send_z(g, slot, partial_sum(g, to), via)
        else:
            for j in (4, 3, 5, 2, 6, 1, 7):
                send_z(g, j, partial_sum(g, j), j)

    def relay(g):
        if g in RELAYED:
            send_z(g, 7, partial_sum(g, -2) + arrived(g, 4), -2)
            send_z(g, 6, partial_sum(g, 2) + arrived(g, 3) + arrived(g, 5), 2)

    def stage_e(g):
        total = partial_sum(g, 0)
        for slot in (1, 2, 7, 6) if g in RELAYED else (1, 7, 2, 6, 3, 5, 4):
            total = total + arrived(g, slot)
        for k in range(g * PER, (g + 1) * PER):
            for i in range(4 // PER):
                q = (k % PER) * (4 // PER) + i
                moved = total if q == 0 else pltpu.roll(total, lane_group - q * feats, 1)
                block = moved[:, :128].astype(BF16)
                if k == 0:
                    ret[k, pl.ds(i * piece_rows, piece_rows)] = block
                else:
                    ys[k, pl.ds(i * piece_rows, piece_rows)] = block
            if k > 0:
                copy = remote(ys.at[k], ret.at[k], g_s.at[k], g_r.at[k], dev_y(OFFSETS[k]))
                copy.start()
                g_copies[k] = copy

    prepare(0, 0, True)
    prepare(0, 1, True)
    share_far(7)
    share_far(5)
    share_far(6)
    to_partner(1)
    prepare(1, c, True)
    to_partner(2)
    prepare(2, c, True)
    prepare_other(1)
    stage_a(0)
    to_partner(7)
    prepare(7, c, True)
    to_partner(6)
    prepare(6, c, True)
    prepare_other(7)
    prepare_other(6)
    stage_a(3)
    to_partner(5)
    prepare(5, c, True)
    to_partner(4)
    prepare(4, c, True)
    prepare_other(5)
    prepare_other(4)
    stage_a(2)
    stage_b(0)
    to_partner(3)
    prepare(3, c, True)
    prepare_other(3)
    prepare_other(2)
    stage_a(1)
    stage_b(3)
    stage_b(2)
    stage_c(0)
    stage_b(1)
    stage_c(3)
    stage_d(0)
    stage_c(2)
    stage_d(3)
    stage_c(1)
    stage_d(2)
    relay(0)
    stage_d(1)
    relay(3)
    relay(2)
    stage_e(0)
    stage_e(3)
    stage_e(2)
    stage_e(1)
    for k in range(1, SLOTS):
        g_copies[k].wait_recv()
    back = ret[...].reshape(SLOTS * rows, 128)
    moe = jnp.dot(pwh[...], back, preferred_element_type=F32)
    moe = moe + jnp.dot(pwl[...], back, preferred_element_type=F32)
    out_ref[...] = (own_ref[:, :feats] + moe[:, :feats]).astype(BF16)
    for group in (a_copies, h_copies, b_copies, c_copies, d_copies, e_copies, f_copies, g_copies):
        for copy in group.values():
            copy.wait_send()


def on_device(tokens, norm_gain, up_w, down_w, expert_ids, gate_gap):
    micro, _, row_count, width = tokens.shape
    n_tok = micro * row_count
    rows = micro * CAP
    units = up_w.shape[2]
    pipe = lax.axis_size("pipe")
    n_z = pipe // 2
    feats = width // pipe
    lane_group = 4 * feats
    piece_rows = PER * rows // 4
    parts = width // lane_group
    flat = tokens.reshape(n_tok, width)
    ids = expert_ids.transpose(0, 1, 3, 2)
    vmem = pl.BlockSpec(memory_space=pltpu.VMEM)
    hbm = pl.BlockSpec(memory_space=pl.ANY)
    dma = pltpu.SemaphoreType.DMA
    result = pl.pallas_call(
        layer_kernel,
        out_shape=jax.ShapeDtypeStruct((n_tok, feats), BF16),
        in_specs=[hbm] * 6,
        out_specs=vmem,
        scratch_shapes=[
            pltpu.VMEM((n_tok, width), BF16),
            pltpu.VMEM((n_tok, 128), F32),
            pltpu.VMEM((width // 128, 128), F32),
            pltpu.VMEM(ids.shape, jnp.int32),
            pltpu.VMEM(gate_gap.shape, F32),
            pltpu.VMEM((width, units), BF16),
            pltpu.VMEM((parts, units, lane_group), BF16),
            pltpu.VMEM((SLOTS, 4, rows // 2, width // 4), BF16),
            pltpu.VMEM((2, SLOTS, 4, rows // 2, width // 4), BF16),
            pltpu.VMEM((GROUPS, PER * rows, width), BF16),
            pltpu.VMEM((GROUPS, 4, piece_rows, units + 128), BF16),
            pltpu.VMEM((GROUPS, 4, piece_rows, units + 128), BF16),
            pltpu.VMEM((GROUPS, 4, piece_rows, units), BF16),
            pltpu.VMEM((GROUPS, 2, n_z, piece_rows, lane_group), BF16),
            pltpu.VMEM((GROUPS, n_z, piece_rows, lane_group), BF16),
            pltpu.VMEM((GROUPS, n_z, piece_rows, lane_group), BF16),
            pltpu.VMEM((GROUPS, n_z, piece_rows, lane_group), BF16),
            pltpu.VMEM((SLOTS, rows, 128), BF16),
            pltpu.VMEM((SLOTS, rows, 128), BF16),
            pltpu.VMEM((n_tok, SLOTS * rows), BF16),
            pltpu.VMEM((n_tok, SLOTS * rows), BF16),
            dma((5 + parts,)),
            dma((SLOTS, 4)), dma((SLOTS, 4)),
            dma((SLOTS,)), dma((SLOTS,)),
            dma((GROUPS, 4)), dma((GROUPS, 4)),
            dma((GROUPS, 4)), dma((GROUPS, 4)),
            dma((GROUPS, parts)), dma((GROUPS, parts)),
            dma((GROUPS, n_z)), dma((GROUPS, n_z)),
            dma((SLOTS,)), dma((SLOTS,)),
        ],
        compiler_params=pltpu.CompilerParams(
            collective_id=0, has_side_effects=True, vmem_limit_bytes=56 * 1024 * 1024
        ),
        name="expert_layer",
    )(flat, norm_gain.reshape(width // 128, 128), ids, gate_gap, up_w[0], down_w[0])
    return result.reshape(micro, 1, row_count, feats)


def solution(mesh):
    return jax.shard_map(
        on_device,
        mesh=mesh,
        in_specs=(
            P(None, "expert", None, "dp"),
            P("dp"),
            P("expert", "dp", "pipe"),
            P("expert", "pipe", "dp"),
            P(None, "expert", None, None),
            P(None, "expert", None),
        ),
        out_specs=P(None, "expert", None, ("dp", "pipe")),
        check_vma=False,
    )
```
